256 devices in a mesh: dp: 4 (over x), rad: 8 (over y, z_lo), azi: 8 (over z_hi, core).
Axes of the slice: x: 4, y: 4, z: 8 (z_hi: 4, z_lo: 2; z = z_hi * 2 + z_lo), core: 2. Of those that a mesh axis runs over, the one named last changes fastest.
Arguments:
- inputs: bfloat16 [4, 96, 32, 64, 256], P('dp', None, 'rad', 'azi'), may hold values from -6 to 6
- weight: bfloat16 [96, 2592], P('dp'), may hold values from -0.125 to 0.125
- bias: bfloat16 [96], P('dp'), may hold values from -3 to 3
- cotangent: bfloat16 [4, 96, 32, 64, 256], P('dp', None, 'rad', 'azi'), may hold values from -6 to 6
Outputs:
- output: bfloat16 [4, 96, 32, 64, 256], P('dp', None, 'rad', 'azi')
- input_grad: bfloat16 [4, 96, 32, 64, 256], P('dp', None, 'rad', 'azi')
- weight_grad: float32 [96, 2592], P('dp')
- bias_grad: float32 [96], P('dp')
The draws below stay inside these ranges and needn't reach their ends.
All inputs are finite; a program needn't handle non-finite values.
Results may differ from the reference program's by a relative error of at most 0.015.
Values may be sent and summed in bfloat16 or wider, within the bound.
No kernel may reach another device: no remote copies, remote signals or barrier semaphores. Data moves between devices by JAX's collectives and lax.ppermute only.
A program may use at most 128 MiB of HBM per device.

```python
import jax
import jax.numpy as jnp
from jax import lax

C = 96
TAPS = 27
NA = 256
BATCH = 4
NR = 32
NT = 64


def shard_levels(key, extent, cuts, low, top_value):
    def one(dim, shards_of):
        steps = jax.random.uniform(jax.random.fold_in(jax.random.fold_in(key, 6), dim), (shards_of,), jnp.float32, low / len(cuts), top_value / len(cuts))
        return jnp.repeat(jnp.exp(steps), extent[dim] // shards_of).reshape((-1,) + (1,) * (len(extent) - dim - 1))

    factor_of = one(*cuts[0])
    for cut in cuts[1:]:
        factor_of = factor_of * one(*cut)
    return factor_of


def noise(key, extent, scale, bound, shards=(), dtype=jnp.bfloat16):
    array = scale * jax.random.normal(key, extent, jnp.float32)
    if shards:
        array = array * shard_levels(key, extent, shards, -0.22, 0.18)
    return jnp.clip(array, -bound, bound).astype(dtype)


def setup_inputs(seed: int = 0) -> dict:
    splits = jax.random.split(jax.random.key(seed), 5)
    return {
        "inputs": noise(splits[0], (BATCH, C, NR, NT, NA), 1.0, 6.0, ((0, 4), (2, 8), (3, 8))),
        "weight": noise(splits[1], (C, TAPS * C), (TAPS * C) ** -0.5, 0.125, ((0, 4),)),
        "bias": noise(splits[2], (C,), 0.5, 3.0, ((0, 4),)),
        "cotangent": noise(splits[3], (BATCH, C, NR, NT, NA), 1.0, 6.0, ((0, 4), (2, 8), (3, 8))),
    }


inverse_scale = 1.0 / 1024.0


def pad_field(field):
    field = jnp.pad(field, ((0, 0), (1, 1), (0, 0), (1, 1)))
    return jnp.concatenate([field[:, :, -1:], field, field[:, :, :1]], axis=2)


def stack_taps(padded, rad_off, azi_off, flipped):
    radial = padded.shape[1] - 2
    azimuth = padded.shape[2] - 2
    axial = padded.shape[3] - 2
    pieces = []
    for tap_k in range(3):
        start_a = 2 - tap_k if flipped else tap_k
        pieces.append(padded[:, rad_off:rad_off + radial, azi_off:azi_off + azimuth, start_a:start_a + axial])
    return jnp.concatenate(pieces, axis=0).astype(jnp.float32)


def reference(inputs, weight, bias, cotangent):
    channels = inputs.shape[1]
    out_rows = weight.shape[0]
    weight_f = weight.astype(jnp.float32)
    high = lax.Precision.HIGHEST

    def per_sample(pair_args):
        sample_in, sample_grad = pair_args
        padded = pad_field(sample_in)
        preact = jnp.zeros((out_rows,) + sample_in.shape[1:], jnp.float32) + bias.astype(jnp.float32)[:, None, None, None]
        for tap_pair in range(9):
            rad_off, azi_off = divmod(tap_pair, 3)
            w_block = weight_f[:, tap_pair * 3 * channels:(tap_pair + 1) * 3 * channels]
            stacked = stack_taps(padded, rad_off, azi_off, False)
            preact = preact + jnp.einsum("om,mrta->orta", w_block, stacked, precision=high)
        gate_value = jax.nn.sigmoid(preact)
        result = (preact * gate_value).astype(jnp.bfloat16)
        delta_z = (sample_grad.astype(jnp.float32) * gate_value * (1.0 + preact * (1.0 - gate_value))).astype(jnp.bfloat16)
        delta_pad = pad_field(delta_z)
        delta_f = delta_z.astype(jnp.float32)
        backward = jnp.zeros(sample_in.shape, jnp.float32)
        pieces = []
        for tap_pair in range(9):
            rad_off, azi_off = divmod(tap_pair, 3)
            w_block = weight_f[:, tap_pair * 3 * channels:(tap_pair + 1) * 3 * channels]
            w_back = w_block.reshape(out_rows, 3, channels).transpose(1, 0, 2).reshape(3 * out_rows, channels)
            dstack = stack_taps(delta_pad, 2 - rad_off, 2 - azi_off, True)
            backward = backward + jnp.einsum("mc,mrta->crta", w_back, dstack, precision=high)
            stacked = stack_taps(padded, rad_off, azi_off, False)
            pieces.append(jnp.einsum("orta,mrta->om", delta_f, stacked, precision=high))
        weight_term = jnp.concatenate(pieces, axis=1)
        bias_term = jnp.sum(delta_f, axis=(1, 2, 3))
        return result, backward.astype(jnp.bfloat16), weight_term, bias_term

    output, input_grad, weight_parts, bias_parts = lax.map(per_sample, (inputs, cotangent))
    weight_grad = jnp.sum(weight_parts, axis=0) * inverse_scale
    bias_grad = jnp.sum(bias_parts, axis=0) * inverse_scale
    return output, input_grad, weight_grad, bias_grad
```

```python
import jax
import jax.numpy as jnp
from jax import lax
from jax.experimental import pallas as pl
from jax.experimental.pallas import tpu as pltpu
from jax.sharding import PartitionSpec as P

inverse_scale = 1.0 / 1024.0
bf16 = jnp.bfloat16
f32 = jnp.float32
C = 96
K9 = 9 * C
RAD_AZI = ("rad", "azi")


def params(*semantics):
    return pltpu.CompilerParams(
        dimension_semantics=semantics, vmem_limit_bytes=56 * 1024 * 1024
    )


def full(shape):
    return pl.BlockSpec(shape, lambda *_: (0,) * len(shape))


def put_rows(tmp, cells):
    c, na, z = cells.shape
    flat = cells.reshape(c * na, z)
    for h in range(z // 128):
        tmp[h] = flat[:, 128 * h : 128 * h + 128]


def get_rows(tmp, c, na):
    flat = jnp.concatenate([tmp[h] for h in range(tmp.shape[0])], axis=1)
    return flat.reshape(c, na, flat.shape[1])


def get_column(tmp, a, c, na):
    return jnp.concatenate(
        [tmp[h, pl.ds(a, c, stride=na), :] for h in range(tmp.shape[0])], axis=1
    )


def put_column(tmp, a, na, column):
    c = column.shape[0]
    for h in range(tmp.shape[0]):
        tmp[h, pl.ds(a, c, stride=na), :] = column[:, 128 * h : 128 * h + 128]


def to_columns_body(x_ref, o_ref, tmp):
    rows, az = x_ref.shape[1], x_ref.shape[3]
    put_rows(tmp, x_ref[0, :, 0].astype(f32))
    for a in range(az):
        o_ref[0, a] = get_column(tmp, a, rows, az).astype(bf16)


def to_columns(field):
    _, c, nr, na, nz = field.shape
    return pl.pallas_call(
        to_columns_body,
        grid=(nr,),
        in_specs=[pl.BlockSpec((1, c, 1, na, nz), lambda r: (0, 0, r, 0, 0))],
        out_specs=pl.BlockSpec((1, na, c, nz), lambda r: (r, 0, 0, 0)),
        out_shape=jax.ShapeDtypeStruct((nr, na, c, nz), bf16),
        scratch_shapes=[pltpu.VMEM((nz // 128, c * na, 128), f32)],
        compiler_params=params("arbitrary"),
        name="to_columns",
    )(field)


def fill(ext, x_ref, lo_ref, hi_ref, left_ref, right_ref):
    nr, na = x_ref.shape[0], x_ref.shape[1]
    ext[0, 1 : na + 1] = lo_ref[...]
    ext[nr + 1, 1 : na + 1] = hi_ref[...]
    for r in range(nr):
        ext[r + 1, 1 : na + 1] = x_ref[r]
    ext[:, 0] = left_ref[...]
    ext[:, na + 1] = right_ref[...]


def window(ext, r, a):
    c, z = ext.shape[2], ext.shape[3]
    return jnp.concatenate(
        [ext[r + i, pl.ds(a, 3)].reshape(3 * c, z) for i in range(3)], axis=0
    )


def taps_sum(parts):
    c = parts.shape[0] // 3
    z = parts.shape[1]
    lane = lax.broadcasted_iota(jnp.int32, (c, z), 1)
    before = jnp.where(lane == 0, 0.0, pltpu.roll(parts[:c], 1, 1))
    after = jnp.where(lane == z - 1, 0.0, pltpu.roll(parts[2 * c :], z - 1, 1))
    return parts[c : 2 * c] + before + after


def forward_body(x_ref, lo_ref, hi_ref, left_ref, right_ref, w_ref, b_ref, cot_ref,
                 out_ref, delta_ref, bsum_ref, ext, cot, res):
    r = pl.program_id(0)
    na, c, z = x_ref.shape[1:]

    @pl.when(r == 0)
    def _():
        fill(ext, x_ref, lo_ref, hi_ref, left_ref, right_ref)
        bsum_ref[...] = jnp.zeros_like(bsum_ref)

    put_rows(cot, cot_ref[0, :, 0].astype(f32))
    bias = b_ref[...].astype(f32)

    def pair(p, carry):
        a = 2 * p
        cols = jnp.concatenate([window(ext, r, a), window(ext, r, a + 1)], axis=1)
        both = jnp.dot(w_ref[...], cols, preferred_element_type=f32)
        for s in range(2):
            pre = taps_sum(both[:, s * z : (s + 1) * z]) + bias
            gate = jax.nn.sigmoid(pre)
            put_column(res, a + s, na, pre * gate)
            d = get_column(cot, a + s, c, na) * gate * (1.0 + pre * (1.0 - gate))
            d = d.astype(bf16)
            delta_ref[0, a + s] = d
            bsum_ref[...] += d.astype(f32)
        return carry

    lax.fori_loop(0, na // 2, pair, 0)
    out_ref[0, :, 0] = get_rows(res, c, na).astype(bf16)


def forward(x, lo, hi, left, right, w, b, cot):
    nr, na, c, z = x.shape
    return pl.pallas_call(
        forward_body,
        grid=(nr,),
        in_specs=[full(x.shape), full(lo.shape), full(hi.shape), full(left.shape),
                  full(right.shape), full(w.shape), full(b.shape),
                  pl.BlockSpec((1, c, 1, na, z), lambda r: (0, 0, r, 0, 0))],
        out_specs=[pl.BlockSpec((1, c, 1, na, z), lambda r: (0, 0, r, 0, 0)),
                   pl.BlockSpec((1, na, c, z), lambda r: (r, 0, 0, 0)),
                   full((c, z))],
        out_shape=[jax.ShapeDtypeStruct(cot.shape, bf16),
                   jax.ShapeDtypeStruct(x.shape, bf16),
                   jax.ShapeDtypeStruct((c, z), f32)],
        scratch_shapes=[pltpu.VMEM((nr + 2, na + 2, c, z), bf16),
                        pltpu.VMEM((z // 128, c * na, 128), f32),
                        pltpu.VMEM((z // 128, c * na, 128), f32)],
        compiler_params=params("arbitrary"),
        name="forward",
    )(x, lo, hi, left, right, w, b, cot)


def backward_body(x_ref, lo_ref, hi_ref, left_ref, right_ref, w_ref, out_ref, ext, res):
    r = pl.program_id(0)
    na, c, z = x_ref.shape[1:]

    @pl.when(r == 0)
    def _():
        fill(ext, x_ref, lo_ref, hi_ref, left_ref, right_ref)

    def pair(p, carry):
        a = 2 * p
        cols = jnp.concatenate([window(ext, r, a), window(ext, r, a + 1)], axis=1)
        both = jnp.dot(w_ref[...], cols, preferred_element_type=f32)
        for s in range(2):
            put_column(res, a + s, na, taps_sum(both[:, s * z : (s + 1) * z]))
        return carry

    lax.fori_loop(0, na // 2, pair, 0)
    out_ref[0, :, 0] = get_rows(res, c, na).astype(bf16)


def backward(x, lo, hi, left, right, w):
    nr, na, c, z = x.shape
    return pl.pallas_call(
        backward_body,
        grid=(nr,),
        in_specs=[full(x.shape), full(lo.shape), full(hi.shape), full(left.shape),
                  full(right.shape), full(w.shape)],
        out_specs=pl.BlockSpec((1, c, 1, na, z), lambda r: (0, 0, r, 0, 0)),
        out_shape=jax.ShapeDtypeStruct((1, c, nr, na, z), bf16),
        scratch_shapes=[pltpu.VMEM((nr + 2, na + 2, c, z), bf16),
                        pltpu.VMEM((z // 128, c * na, 128), f32)],
        compiler_params=params("arbitrary"),
        name="backward",
    )(x, lo, hi, left, right, w)


def weight_body(x_ref, lo_ref, hi_ref, left_ref, right_ref, d_ref, bsum_ref, out_ref,
                ext, acc, flat):
    r = pl.program_id(0)
    nr, na, c, z = x_ref.shape

    @pl.when(r == 0)
    def _():
        fill(ext, x_ref, lo_ref, hi_ref, left_ref, right_ref)
        acc[...] = jnp.zeros_like(acc)

    lane = lax.broadcasted_iota(jnp.int32, (c, z), 1)

    def pair(p, carry):
        a = 2 * p
        cols = jnp.concatenate([window(ext, r, a), window(ext, r, a + 1)], axis=1)
        rows = []
        for s in range(2):
            d = d_ref[r, a + s].astype(f32)
            ahead = jnp.where(lane == z - 1, 0.0, pltpu.roll(d, z - 1, 1))
            behind = jnp.where(lane == 0, 0.0, pltpu.roll(d, 1, 1))
            rows.append(jnp.concatenate([ahead, d, behind], axis=0).astype(bf16))
        rows = jnp.concatenate(rows, axis=1)
        acc[...] += lax.dot_general(rows, cols, (((1,), (1,)), ((), ())),
                                    preferred_element_type=f32)
        return carry

    lax.fori_loop(0, na // 2, pair, 0)

    @pl.when(r == nr - 1)
    def _():
        flat[...] = jnp.zeros_like(flat)
        for ij in range(9):
            for k in range(3):
                t = 3 * ij + k
                flat[:, t * c : (t + 1) * c] = acc[k * c : (k + 1) * c, ij * c : (ij + 1) * c]
        flat[:, 27 * c : 27 * c + 1] = jnp.sum(bsum_ref[...], axis=1, keepdims=True)
        for g in range(c // 8):
            for l in range(21):
                out_ref[g // 3, (g % 3) * 21 + l] = (
                    flat[8 * g : 8 * g + 8, 128 * l : 128 * l + 128] * inverse_scale
                ).astype(bf16)
        out_ref[:, 63] = jnp.zeros((4, 8, 128), bf16)


def weight_terms(x, lo, hi, left, right, d, bsum):
    nr, na, c, z = x.shape
    return pl.pallas_call(
        weight_body,
        grid=(nr,),
        in_specs=[full(x.shape), full(lo.shape), full(hi.shape), full(left.shape),
                  full(right.shape), full(d.shape), full(bsum.shape)],
        out_specs=full((4, 64, 8, 128)),
        out_shape=jax.ShapeDtypeStruct((4, 64, 8, 128), bf16),
        scratch_shapes=[pltpu.VMEM((nr + 2, na + 2, c, z), bf16),
                        pltpu.VMEM((3 * c, K9), f32),
                        pltpu.VMEM((c, 21 * 128), f32)],
        compiler_params=params("arbitrary"),
        name="weight_terms",
    )(x, lo, hi, left, right, d, bsum)


def rad_shift(x, step):
    n = lax.axis_size("rad")
    return lax.ppermute(x, "rad", [(i, i + step) for i in range(n) if 0 <= i + step < n])


def azi_shift(x, step):
    n = lax.axis_size("azi")
    return lax.ppermute(x, "azi", [(i, (i + step) % n) for i in range(n)])


def halos(x):
    hi = rad_shift(x[0], -1)
    lo = rad_shift(x[-1], 1)
    first = jnp.concatenate([lo[:1], x[:, 0], hi[:1]], axis=0)
    last = jnp.concatenate([lo[-1:], x[:, -1], hi[-1:]], axis=0)
    right = azi_shift(first, -1)
    left = azi_shift(last, 1)
    return lo, hi, left, right


def exchange(x, axis):
    return lax.all_to_all(x, axis, 0, 0, tiled=True)


def reduce_terms(tiles):
    def total(x, parts):
        return jnp.sum(x.reshape((parts, -1) + x.shape[1:]).astype(f32), axis=0)

    mine = total(exchange(tiles.reshape(256, 8, 128), "dp"), 4).astype(bf16)
    piece = total(exchange(mine, RAD_AZI), 64).astype(bf16)
    return exchange(jnp.broadcast_to(piece, (64, 8, 128)), RAD_AZI)


def on_device(inputs, weight, bias, cotangent):
    c = inputs.shape[1]
    x = to_columns(inputs)
    packed = jnp.concatenate(
        [weight, jnp.broadcast_to(bias[:, None], (weight.shape[0], 128))], axis=1
    )
    rows = packed.shape[0]
    d0 = lax.axis_index("dp")
    pieces = [packed] + [
        lax.ppermute(packed, "dp", [(i, (i + s) % 4) for i in range(4)]) for s in (1, 2, 3)
    ]
    stacked = jnp.stack(pieces)
    order = (d0 - jnp.arange(4)) % 4
    whole = stacked[order].reshape(4 * rows, packed.shape[1])
    taps = whole[:, : 27 * c].reshape(c, 3, 3, 3, c)
    w_fwd = taps.transpose(3, 0, 1, 2, 4).reshape(3 * c, K9)
    w_back = taps[:, ::-1, ::-1, ::-1].transpose(3, 4, 1, 2, 0).reshape(3 * c, K9)
    b_col = whole[:, 27 * c : 27 * c + 1]

    lo, hi, left, right = halos(x)
    output, delta, bsum = forward(x, lo, hi, left, right, w_fwd, b_col, cotangent)
    dlo, dhi, dleft, dright = halos(delta)
    terms = weight_terms(x, lo, hi, left, right, delta, bsum)
    input_grad = backward(delta, dlo, dhi, dleft, dright, w_back)
    tiles = reduce_terms(terms)
    summed = tiles[:63].reshape(3, 21, 8, 128).transpose(0, 2, 1, 3).reshape(24, 21 * 128)
    summed = summed.astype(f32)
    return output, input_grad, summed[:, : 27 * c], summed[:, 27 * c]


def solution(mesh):
    return jax.shard_map(
        on_device,
        mesh=mesh,
        in_specs=(
            P("dp", None, "rad", "azi", None),
            P("dp", None),
            P("dp"),
            P("dp", None, "rad", "azi", None),
        ),
        out_specs=(
            P("dp", None, "rad", "azi", None),
            P("dp", None, "rad", "azi", None),
            P("dp", None),
            P("dp"),
        ),
        check_vma=False,
    )
```

```python
import jax
import jax.numpy as jnp
from jax import lax
from jax.experimental import pallas as pl
from jax.experimental.pallas import tpu as pltpu
from jax.sharding import PartitionSpec as P


inverse_scale = 1.0 / 1024.0
bf16 = jnp.bfloat16
f32 = jnp.float32
C = 96
K9 = 9 * C


def full(x):
    return pl.BlockSpec(x.shape, lambda *_: (0,) * len(x.shape))


def shape(dims, dtype=bf16):
    return jax.ShapeDtypeStruct(dims, dtype)


def call(body, place, grid, args, in_specs, outs, out_specs, scratch, cost, alias=None):
    return pl.pallas_call(
        body,
        grid_spec=pltpu.PrefetchScalarGridSpec(
            num_scalar_prefetch=1, grid=(grid,), in_specs=in_specs, out_specs=out_specs,
            scratch_shapes=scratch),
        out_shape=outs,
        input_output_aliases=alias or {},
        compiler_params=pltpu.CompilerParams(
            dimension_semantics=("arbitrary",), vmem_limit_bytes=56 * 1024 * 1024),
        cost_estimate=pl.CostEstimate(flops=cost, transcendentals=0, bytes_accessed=4000000),
    )(place, *args)


def put_rows(tmp, cells):
    c, na, z = cells.shape
    flat = cells.reshape(c * na, z)
    for h in range(z // 128):
        tmp[h] = flat[:, 128 * h : 128 * h + 128]


def get_rows(tmp, c, na):
    flat = jnp.concatenate([tmp[h] for h in range(tmp.shape[0])], axis=1)
    return flat.reshape(c, na, flat.shape[1])


def get_column(tmp, a, c, na):
    return jnp.concatenate(
        [tmp[h, pl.ds(a, c, stride=na), :] for h in range(tmp.shape[0])], axis=1
    )


def put_column(tmp, a, na, column):
    c = column.shape[0]
    for h in range(tmp.shape[0]):
        tmp[h, pl.ds(a, c, stride=na), :] = column[:, 128 * h : 128 * h + 128]


def columns_body(place, x_ref, o_ref, near_ref, far_ref, tmp):
    c, nr, na = x_ref.shape[1:4]
    p = place[0]
    for r in range(nr):
        put_rows(tmp, x_ref[0, :, r].astype(f32))
        for a in range(na):
            o_ref[r, a] = get_column(tmp, a, c, na).astype(bf16)
        near_ref[r] = o_ref[r, (na - 1) * (1 - p)]
        far_ref[r] = o_ref[r, (na - 1) * p]


def to_columns(place, field):
    _, c, nr, na, nz = field.shape
    face = shape((nr, c, nz))
    part = c // 3
    face_spec = pl.BlockSpec((nr, part, nz), lambda g, _: (0, g, 0))
    return call(
        columns_body, place, 3, (field,),
        [pl.BlockSpec((1, part, nr, na, nz), lambda g, _: (0, g, 0, 0, 0))],
        [shape((nr, na, c, nz)), face, face],
        [pl.BlockSpec((nr, na, part, nz), lambda g, _: (0, 0, g, 0)), face_spec, face_spec],
        [pltpu.VMEM((nz // 128, part * na, 128), f32)], 10000000)


ANY = pl.BlockSpec(memory_space=pl.ANY)


def edges_body(place, rows, near, far, out_near, out_far, buf, sems):
    p, q = place[0], place[1]
    last, na = rows.shape[0] - 1, rows.shape[1]
    right, left = (na + 1) * (1 - p), (na + 1) * p
    step = (near.shape[0] - 1) // last
    loads = []
    for k, r in enumerate((last * (1 - q), last * q)):
        for n, (src, dst) in enumerate((
            (rows.at[r], buf.at[k, pl.ds(1, na)]),
            (near.at[step * r], buf.at[k, right]),
            (far.at[step * r], buf.at[k, left]),
        )):
            loads.append(pltpu.make_async_copy(src, dst, sems.at[k, n]))
    stores = [pltpu.make_async_copy(buf.at[k], out, sems.at[k, 3])
              for k, out in enumerate((out_near, out_far))]
    for copy in loads:
        copy.start()
    for k, store in enumerate(stores):
        for copy in loads[3 * k : 3 * k + 3]:
            copy.wait()
        store.start()
    for store in stores:
        store.wait()


def edges(place, rows, near, far):
    _, na, c, z = rows.shape
    out = shape((na + 2, c, z))
    return call(
        edges_body, place, 1, (rows, near, far), [ANY, ANY, ANY], [out, out],
        [ANY, ANY], [pltpu.VMEM((2, na + 2, c, z), bf16), pltpu.SemaphoreType.DMA((2, 4))],
        1000000)


class Loader:
    def __init__(self, ext, sems, place, rows, sides, ends=()):
        p, q = place[0], place[1]
        self.ext, self.sems, self.ends = ext, sems, ends
        na = ext.shape[1] - 2
        self.own = {}
        for e in range(1, 5):
            if len(rows) == 1:
                row = rows[0].at[e - 1]
            else:
                row = rows[0].at[e - 2] if e in (2, 3) else rows[1].at[0 if e == 1 else 1]
            self.own[e] = [
                pltpu.make_async_copy(row, ext.at[e, pl.ds(1, na)], sems.at[e, 0]),
                pltpu.make_async_copy(sides[0].at[e - 1], ext.at[e, (na + 1) * (1 - p)],
                                      sems.at[e, 1]),
                pltpu.make_async_copy(sides[1].at[e - 1], ext.at[e, (na + 1) * p],
                                      sems.at[e, 2]),
            ]
        self.q = q

    def end(self, k, e):
        return pltpu.make_async_copy(self.ends[k], self.ext.at[e], self.sems.at[e, 0])

    def start(self):
        if self.ends:
            self.end(0, 5 * (1 - self.q)).start()
            self.end(1, 5 * self.q).start()
        for e in range(1, 5):
            for copy in self.own[e]:
                copy.start()

    def wait(self, *rows):
        for e in rows:
            if e in (0, 5):
                self.end(0, e).wait()
            else:
                for copy in self.own[e]:
                    copy.wait()

    def step(self, g):
        first, second = ((0, 1, 2), (3, 4, 5)) if self.ends else ((1, 2, 3), (4,))

        @pl.when(g == 0)
        def _():
            self.start()
            self.wait(*first)

        pl.when(g == 1)(lambda: self.wait(*second))

    def all_rows(self, g):
        @pl.when(g == 0)
        def _():
            self.start()
            self.wait(0, 1, 2)

        for k in (1, 2, 3):
            pl.when(g == k)(lambda k=k: self.wait(k + 2))


def ext_scratch(na, c, z):
    return [pltpu.VMEM((6, na + 2, c, z), bf16), pltpu.SemaphoreType.DMA((6, 3))]


def window(ext, r, a):
    c, z = ext.shape[2], ext.shape[3]
    return jnp.concatenate(
        [ext[r + i, pl.ds(a, 3)].reshape(3 * c, z) for i in range(3)], axis=0
    )


def taps_sum(parts):
    c = parts.shape[0] // 3
    z = parts.shape[1]
    lane = lax.broadcasted_iota(jnp.int32, (c, z), 1)
    before = jnp.where(lane == 0, 0.0, pltpu.roll(parts[:c], 1, 1))
    after = jnp.where(lane == z - 1, 0.0, pltpu.roll(parts[2 * c :], z - 1, 1))
    return parts[c : 2 * c] + before + after


def forward_column(pre, cot, res, a, na):
    gate = jax.nn.sigmoid(pre)
    put_column(res, a, na, pre * gate)
    d = get_column(cot, a, pre.shape[0], na) * gate * (1.0 + pre * (1.0 - gate))
    return d.astype(bf16)


def shifted(d):
    c, z = d.shape
    lane = lax.broadcasted_iota(jnp.int32, (c, z), 1)
    d = d.astype(f32)
    ahead = jnp.where(lane == z - 1, 0.0, pltpu.roll(d, z - 1, 1))
    behind = jnp.where(lane == 0, 0.0, pltpu.roll(d, 1, 1))
    return jnp.concatenate([ahead, d, behind], axis=0).astype(bf16)


def forward_body(outer, place, x_ref, *refs):
    sides, refs = refs[:2], refs[2:]
    ends = ()
    if outer:
        ends, refs = refs[:2], refs[2:]
    w_ref, b_ref, cot_ref, *refs = refs
    if outer:
        _, near_in, far_in, bsum, acc_in, *refs = refs
        (out_ref, delta_ref, near_ref, far_ref, keep_ref, send_ref,
         ext, sems, cot, res, acc, total, flat, acc_sem) = refs
    else:
        out_ref, delta_ref, near_ref, far_ref, total, acc, ext, sems, cot, res = refs
    g = pl.program_id(0)
    r = 3 * g if outer else 1 + g
    p = place[0]
    _, na, c, z = x_ref.shape
    if outer:
        bring = pltpu.make_async_copy(acc_in, acc, acc_sem)
        pl.when(g == 0)(lambda: bring.start())
    Loader(ext, sems, place, [x_ref], sides, ends).step(g)

    @pl.when(g == 0)
    def _():
        if outer:
            total[...] = bsum[...]
            near_ref[1:3] = near_in[...]
            far_ref[1:3] = far_in[...]
            bring.wait()
        else:
            total[...] = jnp.zeros_like(total)
            acc[...] = jnp.zeros_like(acc)

    put_rows(cot, cot_ref[0, :, 0].astype(f32))
    bias = b_ref[...].astype(f32)

    def pair(k, carry):
        a = 2 * k
        cols = jnp.concatenate([window(ext, r, a), window(ext, r, a + 1)], axis=1)
        both = jnp.dot(w_ref[...], cols, preferred_element_type=f32)
        rows = []
        for s in range(2):
            pre = taps_sum(both[:, s * z : (s + 1) * z]) + bias
            d = forward_column(pre, cot, res, a + s, na)
            delta_ref[0, a + s] = d
            total[...] += d.astype(f32)
            rows.append(shifted(d))
        acc[...] += lax.dot_general(jnp.concatenate(rows, axis=1), cols,
                                    (((1,), (1,)), ((), ())), preferred_element_type=f32)
        return carry

    lax.fori_loop(0, na // 2, pair, 0)
    out_ref[0, :, 0] = get_rows(res, c, na).astype(bf16)
    slot = r if outer else g
    near_ref[slot] = delta_ref[0, (na - 1) * (1 - p)]
    far_ref[slot] = delta_ref[0, (na - 1) * p]
    if not outer:
        return

    def tiles(low, high):
        for s in range(4):
            first = 24 * ((place[2] + s) % 4)
            for b in range(3):
                rows = pl.ds(pl.multiple_of(first + 8 * b, 8), 8)
                for l in range(21):
                    n = b * 21 + l
                    (low if n < 32 else high)[s, n % 32] = (
                        flat[rows, 128 * l : 128 * l + 128] * inverse_scale
                    ).astype(bf16)
            high[s, 31] = jnp.zeros((8, 128), bf16)

    @pl.when(g == 1)
    def _():
        flat[:, 27 * c :] = jnp.zeros((c, flat.shape[1] - 27 * c), f32)
        for ij in range(9):
            for k in range(3):
                t = 3 * ij + k
                flat[:, t * c : (t + 1) * c] = acc[k * c : (k + 1) * c, ij * c : (ij + 1) * c]
        flat[:, 27 * c : 27 * c + 1] = jnp.sum(total[...], axis=1, keepdims=True)
        pl.when(p == 0)(lambda: tiles(keep_ref, send_ref))
        pl.when(p == 1)(lambda: tiles(send_ref, keep_ref))


def forward(place, x, sides, ends, w, b, cot, before=None):
    _, na, c, z = x.shape
    outer = before is not None
    field = pl.BlockSpec(
        (1, c, 1, na, z), lambda g, _: (0, 0, 3 * g if outer else 1 + g, 0, 0))
    args = [x, *sides, *ends, w, b, cot]
    specs = [ANY] * (3 + len(ends)) + [full(w), full(b), field]
    face = shape((4 if outer else 2, c, z))
    bsum, acc = shape((c, z), f32), shape((3 * c, K9), f32)
    half = shape((4, 32, 8, 128))
    rest = [face, face] + ([half, half] if outer else [bsum, acc])
    scratch = ext_scratch(na, c, z) + [pltpu.VMEM((z // 128, c * na, 128), f32)] * 2
    alias = None
    if outer:
        alias = {1 + len(args): 0}
        specs += [ANY] + [full(y) for y in before[1:4]] + [ANY]
        args += before
        scratch += [pltpu.VMEM(acc.shape, f32), pltpu.VMEM(bsum.shape, f32),
                    pltpu.VMEM((c, 21 * 128), f32), pltpu.SemaphoreType.DMA]
    return call(
        lambda *refs: forward_body(outer, *refs), place, 2,
        args, specs, [shape(cot.shape), shape((2, na, c, z))] + rest,
        [field, pl.BlockSpec((1, na, c, z), lambda g, _: (g, 0, 0, 0))]
        + [full(y) for y in rest],
        scratch, 5000000000, alias)


def backward_body(place, d_in, d_out, *refs):
    sides, ends = refs[:2], refs[2:4]
    w_ref, out_ref, ext, sems, res = refs[4:]
    r = pl.program_id(0)
    _, na, c, z = d_in.shape
    Loader(ext, sems, place, [d_in, d_out], sides, ends).all_rows(r)

    def pair(k, carry):
        a = 2 * k
        cols = jnp.concatenate([window(ext, r, a), window(ext, r, a + 1)], axis=1)
        both = jnp.dot(w_ref[...], cols, preferred_element_type=f32)
        for s in range(2):
            put_column(res, a + s, na, taps_sum(both[:, s * z : (s + 1) * z]))
        return carry

    lax.fori_loop(0, na // 2, pair, 0)
    out_ref[0, :, 0] = get_rows(res, c, na).astype(bf16)


def backward(place, d_in, d_out, sides, ends, w):
    _, na, c, z = d_in.shape
    return call(
        backward_body, place, 4, [d_in, d_out, *sides, *ends, w],
        [ANY] * 6 + [full(w)], shape((1, c, 4, na, z)),
        pl.BlockSpec((1, c, 1, na, z), lambda r, _: (0, 0, r, 0, 0)),
        ext_scratch(na, c, z) + [pltpu.VMEM((z // 128, c * na, 128), f32)], 5000000000)


def near_pairs(axis):
    return [(i, i ^ 1) for i in range(lax.axis_size(axis))]


def far_pairs(axis):
    n = lax.axis_size(axis)
    pairs = [(i, i - 1 if i % 2 == 0 else i + 1) for i in range(n)]
    if axis == "azi":
        return [(i, j % n) for i, j in pairs]
    return [(i, j) for i, j in pairs if 0 <= j < n]


def swap(x, axis):
    near, far = x
    got_far = lax.ppermute(far, axis, far_pairs(axis))
    got_near = lax.ppermute(near, axis, near_pairs(axis))
    return got_near, got_far


def sum_over(x, axis, step):
    n = lax.axis_size(axis)
    parts = [x] + [
        lax.ppermute(x, axis, [(i, (i + step * s) % n) for i in range(n)]) for s in (1, 2, 3)
    ]
    a, b, c, d = (y.astype(f32) for y in parts)
    return (a + c) + (b + d)


def reduce_terms(keep, send):
    core = [(i, i ^ 1) for i in range(lax.axis_size("azi"))]
    got = lax.ppermute(send, "azi", core)
    mine = [keep[s].astype(f32) + got[s].astype(f32) for s in range(4)]
    total = mine[0]
    for s in (1, 2, 3):
        y = lax.ppermute(mine[s].astype(bf16), "dp", [(i, (i + s) % 4) for i in range(4)])
        total = total + y.astype(f32)
    n = lax.axis_size("rad")
    for step in (2, 4):
        total = total.astype(bf16)
        y = lax.ppermute(total, "rad", [(i, i ^ step) for i in range(n)])
        total = total.astype(f32) + y.astype(f32)
    total = sum_over(total.astype(bf16), "azi", 2).astype(bf16)
    y = lax.ppermute(total, "rad", [(i, i ^ 1) for i in range(lax.axis_size("rad"))])
    total = total.astype(f32) + y.astype(f32)
    y = lax.ppermute(total, "azi", core)
    low = lax.axis_index("azi") % 2 == 0
    return jnp.concatenate([jnp.where(low, total, y), jnp.where(low, y, total)], axis=0)


def whole_weights(weight, bias):
    rows, width = weight.shape
    packed = jnp.concatenate([weight, jnp.broadcast_to(bias[:, None], (rows, 128))], axis=1)
    pieces = [packed] + [
        lax.ppermute(packed, "dp", [(i, (i + s) % 4) for i in range(4)]) for s in (1, 2, 3)
    ]
    order = (lax.axis_index("dp") - jnp.arange(4)) % 4
    whole = jnp.stack(pieces)[order].reshape(4 * rows, packed.shape[1])
    taps = whole[:, :width].reshape(4 * rows, 3, 3, 3, C)
    w_fwd = taps.transpose(3, 0, 1, 2, 4).reshape(3 * C, K9)
    w_back = taps[:, ::-1, ::-1, ::-1].transpose(3, 4, 1, 2, 0).reshape(3 * C, K9)
    return w_fwd, w_back, whole[:, width : width + 1]


def on_device(inputs, weight, bias, cotangent):
    place = jnp.stack(
        [lax.axis_index("azi") % 2, lax.axis_index("rad") % 2, lax.axis_index("dp")]
    ).astype(jnp.int32)
    x, near_face, far_face = to_columns(place, inputs)
    sides = swap((near_face, far_face), "azi")
    ends = swap(edges(place, x, *sides), "rad")
    w_fwd, w_back, b_col = whole_weights(weight, bias)
    out, d_in, near_in, far_in, bsum, acc = forward(
        place, x, sides, (), w_fwd, b_col, cotangent)
    output, d_out, near_face, far_face, keep, send = forward(
        place, x, sides, ends, w_fwd, b_col, cotangent, [out, near_in, far_in, bsum, acc])
    d_sides = swap((near_face, far_face), "azi")
    d_ends = swap(edges(place, d_out, *d_sides), "rad")
    tiles = reduce_terms(keep, send)
    input_grad = backward(place, d_in, d_out, d_sides, d_ends, w_back)
    summed = tiles[:63].reshape(3, 21, 8, 128).transpose(0, 2, 1, 3).reshape(24, 21 * 128)
    return output, input_grad, summed[:, : 27 * C], summed[:, 27 * C]


def solution(mesh):
    return jax.shard_map(
        on_device,
        mesh=mesh,
        in_specs=(
            P("dp", None, "rad", "azi", None),
            P("dp", None),
            P("dp"),
            P("dp", None, "rad", "azi", None),
        ),
        out_specs=(
            P("dp", None, "rad", "azi", None),
            P("dp", None, "rad", "azi", None),
            P("dp", None),
            P("dp"),
        ),
        check_vma=False,
    )
```

```python
import jax
import jax.numpy as jnp
from jax import lax
from jax.experimental import pallas as pl
from jax.experimental.pallas import tpu as pltpu
from jax.sharding import PartitionSpec as P


inverse_scale = 1.0 / 1024.0
bf16 = jnp.bfloat16
f32 = jnp.float32
C = 96
K9 = 9 * C


def full(x):
    return pl.BlockSpec(x.shape, lambda *_: (0,) * len(x.shape))


def shape(dims, dtype=bf16):
    return jax.ShapeDtypeStruct(dims, dtype)


def call(body, place, grid, args, in_specs, outs, out_specs, scratch, cost, alias=None):
    return pl.pallas_call(
        body,
        grid_spec=pltpu.PrefetchScalarGridSpec(
            num_scalar_prefetch=1, grid=(grid,), in_specs=in_specs, out_specs=out_specs,
            scratch_shapes=scratch),
        out_shape=outs,
        input_output_aliases=alias or {},
        compiler_params=pltpu.CompilerParams(
            dimension_semantics=("arbitrary",), vmem_limit_bytes=56 * 1024 * 1024),
        cost_estimate=pl.CostEstimate(flops=cost, transcendentals=0, bytes_accessed=4000000),
    )(place, *args)


def put_rows(tmp, cells):
    c, na, z = cells.shape
    flat = cells.reshape(c * na, z)
    for h in range(z // 128):
        tmp[h] = flat[:, 128 * h : 128 * h + 128]


def get_rows(tmp, c, na):
    flat = jnp.concatenate([tmp[h] for h in range(tmp.shape[0])], axis=1)
    return flat.reshape(c, na, flat.shape[1])


def get_column(tmp, a, c, na):
    return jnp.concatenate(
        [tmp[h, pl.ds(a, c, stride=na), :] for h in range(tmp.shape[0])], axis=1
    )


def put_column(tmp, a, na, column):
    c = column.shape[0]
    for h in range(tmp.shape[0]):
        tmp[h, pl.ds(a, c, stride=na), :] = column[:, 128 * h : 128 * h + 128]


def columns_body(place, x_ref, o_ref, near_ref, far_ref, tmp):
    c, nr, na = x_ref.shape[1:4]
    p = place[0]
    for r in range(nr):
        put_rows(tmp, x_ref[0, :, r].astype(f32))
        for a in range(na):
            o_ref[r, a] = get_column(tmp, a, c, na).astype(bf16)
        near_ref[r] = o_ref[r, (na - 1) * (1 - p)]
        far_ref[r] = o_ref[r, (na - 1) * p]


def to_columns(place, field):
    _, c, nr, na, nz = field.shape
    face = shape((nr, c, nz))
    part = c // 3
    face_spec = pl.BlockSpec((nr, part, nz), lambda g, _: (0, g, 0))
    return call(
        columns_body, place, 3, (field,),
        [pl.BlockSpec((1, part, nr, na, nz), lambda g, _: (0, g, 0, 0, 0))],
        [shape((nr, na, c, nz)), face, face],
        [pl.BlockSpec((nr, na, part, nz), lambda g, _: (0, 0, g, 0)), face_spec, face_spec],
        [pltpu.VMEM((nz // 128, part * na, 128), f32)], 10000000)


ANY = pl.BlockSpec(memory_space=pl.ANY)


def edges_body(place, rows, near, far, out_near, out_far, buf, sems):
    p, q = place[0], place[1]
    last, na = rows.shape[0] - 1, rows.shape[1]
    right, left = (na + 1) * (1 - p), (na + 1) * p
    step = (near.shape[0] - 1) // last
    loads = []
    for k, r in enumerate((last * (1 - q), last * q)):
        for n, (src, dst) in enumerate((
            (rows.at[r], buf.at[k, pl.ds(1, na)]),
            (near.at[step * r], buf.at[k, right]),
            (far.at[step * r], buf.at[k, left]),
        )):
            loads.append(pltpu.make_async_copy(src, dst, sems.at[k, n]))
    stores = [pltpu.make_async_copy(buf.at[k], out, sems.at[k, 3])
              for k, out in enumerate((out_near, out_far))]
    for copy in loads:
        copy.start()
    for k, store in enumerate(stores):
        for copy in loads[3 * k : 3 * k + 3]:
            copy.wait()
        store.start()
    for store in stores:
        store.wait()


def edges(place, rows, near, far):
    _, na, c, z = rows.shape
    out = shape((na + 2, c, z))
    return call(
        edges_body, place, 1, (rows, near, far), [ANY, ANY, ANY], [out, out],
        [ANY, ANY], [pltpu.VMEM((2, na + 2, c, z), bf16), pltpu.SemaphoreType.DMA((2, 4))],
        1000000)


def sides_body(place, near_face, far_face, near_end, far_end, out_near, out_far, buf, sems):
    p, q = place[0], place[1]
    last = near_end.shape[0] - 1
    loads = []
    for k, (face, col) in enumerate(((near_face, last * (1 - p)), (far_face, last * p))):
        for n, (src, dst) in enumerate((
            (face, buf.at[k, pl.ds(1, 4)]),
            (near_end.at[col], buf.at[k, 5 * (1 - q)]),
            (far_end.at[col], buf.at[k, 5 * q]),
        )):
            loads.append(pltpu.make_async_copy(src, dst, sems.at[k, n]))
    stores = [pltpu.make_async_copy(buf.at[k], out, sems.at[k, 3])
              for k, out in enumerate((out_near, out_far))]
    for copy in loads:
        copy.start()
    for k, store in enumerate(stores):
        for copy in loads[3 * k : 3 * k + 3]:
            copy.wait()
        store.start()
    for store in stores:
        store.wait()


def six_rows(place, near_face, far_face, ends):
    _, c, z = ends[0].shape
    out = shape((6, c, z))
    return call(
        sides_body, place, 1, (near_face, far_face, *ends), [ANY] * 4, [out, out],
        [ANY, ANY], [pltpu.VMEM((2, 6, c, z), bf16), pltpu.SemaphoreType.DMA((2, 4))],
        1000000)


class Loader:
    def __init__(self, ext, sems, place, rows, sides, ends, w, w_buf):
        p, q = place[0], place[1]
        self.w = pltpu.make_async_copy(w, w_buf, sems.at[0, 3])
        self.ext, self.sems, self.ends = ext, sems, ends
        na = ext.shape[1] - 2
        six = sides[0].shape[0] == 6
        self.own = {}
        for e in range(6):
            copies = []
            if e in (0, 5):
                if not ends:
                    continue
            elif len(rows) == 1:
                copies.append(pltpu.make_async_copy(
                    rows[0].at[e - 1], ext.at[e, pl.ds(1, na)], sems.at[e, 0]))
            else:
                row = rows[0].at[e - 2] if e in (2, 3) else rows[1].at[0 if e == 1 else 1]
                copies.append(pltpu.make_async_copy(row, ext.at[e, pl.ds(1, na)], sems.at[e, 0]))
            if six or e not in (0, 5):
                for k, col in enumerate(((na + 1) * (1 - p), (na + 1) * p)):
                    copies.append(pltpu.make_async_copy(
                        sides[k].at[e if six else e - 1], ext.at[e, col], sems.at[e, 1 + k]))
            self.own[e] = copies
        self.q = q

    def end(self, k, e):
        dst = self.ext.at[e]
        if self.ends[k].shape[0] < self.ext.shape[1]:
            dst = self.ext.at[e, pl.ds(1, self.ends[k].shape[0])]
        return pltpu.make_async_copy(self.ends[k], dst, self.sems.at[e, 0])

    def start(self):
        for e in (1, 2):
            for copy in self.own[e]:
                copy.start()
        if self.ends:
            self.end(0, 5 * (1 - self.q)).start()
            self.end(1, 5 * self.q).start()
        self.w.start()
        for e in (0, 5, 3, 4):
            for copy in self.own.get(e, ()):
                copy.start()

    def wait(self, *rows):
        for e in rows:
            if e in (0, 5):
                self.end(0, e).wait()
            for copy in self.own[e]:
                copy.wait()

    def step(self, g):
        first, second = ((0, 1, 2), (3, 4, 5)) if self.ends else ((1, 2, 3), (4,))

        @pl.when(g == 0)
        def _():
            self.start()
            self.wait(*first)
            self.w.wait()

        pl.when(g == 1)(lambda: self.wait(*second))

    def each(self, r):
        @pl.when(r == 0)
        def _():
            self.start()
            self.wait(0, 1, 2)
            self.w.wait()

        for k in (1, 2, 3):
            pl.when(r == k)(lambda k=k: self.wait(k + 2))


def ext_scratch(na, c, z):
    return [pltpu.VMEM((6, na + 2, c, z), bf16), pltpu.SemaphoreType.DMA((6, 5)),
            pltpu.VMEM((3 * c, K9), bf16)]


def window(ext, r, a):
    c, z = ext.shape[2], ext.shape[3]
    return jnp.concatenate(
        [ext[r + i, pl.ds(a, 3)].reshape(3 * c, z) for i in range(3)], axis=0
    )


def taps_sum(parts):
    c = parts.shape[0] // 3
    z = parts.shape[1]
    lane = lax.broadcasted_iota(jnp.int32, (c, z), 1)
    before = jnp.where(lane == 0, 0.0, pltpu.roll(parts[:c], 1, 1))
    after = jnp.where(lane == z - 1, 0.0, pltpu.roll(parts[2 * c :], z - 1, 1))
    return parts[c : 2 * c] + before + after


def forward_column(pre, cot, res, a, na):
    gate = jax.nn.sigmoid(pre)
    put_column(res, a, na, pre * gate)
    d = get_column(cot, a, pre.shape[0], na) * gate * (1.0 + pre * (1.0 - gate))
    return d.astype(bf16)


def shifted(d):
    c, z = d.shape
    lane = lax.broadcasted_iota(jnp.int32, (c, z), 1)
    d = d.astype(f32)
    ahead = jnp.where(lane == z - 1, 0.0, pltpu.roll(d, z - 1, 1))
    behind = jnp.where(lane == 0, 0.0, pltpu.roll(d, 1, 1))
    return jnp.concatenate([ahead, d, behind], axis=0).astype(bf16)


def forward_body(outer, place, x_ref, *refs):
    sides, refs = refs[:2], refs[2:]
    ends = ()
    if outer:
        ends, refs = refs[:2], refs[2:]
    w_ref, b_ref, cot_ref, *refs = refs
    if outer:
        _, near_in, far_in, bsum_in, *refs = refs
        (out_ref, delta_ref, near_ref, far_ref, total, near_row, far_row,
         ext, sems, w_buf, cot, res, cot_buf, b_buf) = refs
    else:
        (out_ref, delta_ref, near_ref, far_ref, total, acc,
         ext, sems, w_buf, cot, res, cot_buf, b_buf) = refs
    g = pl.program_id(0)
    r = 3 * g if outer else 1 + g
    p, q = place[0], place[1]
    _, na, c, z = x_ref.shape
    cots = [
        pltpu.make_async_copy(cot_ref.at[0, :, 3 * k if outer else 1 + k], cot_buf.at[k],
                              sems.at[1 + k, 3])
        for k in range(2)
    ]
    small = [pltpu.make_async_copy(b_ref, b_buf, sems.at[3, 3])]
    if outer:
        small += [
            pltpu.make_async_copy(near_in, near_ref.at[pl.ds(1, 2)], sems.at[4, 3]),
            pltpu.make_async_copy(far_in, far_ref.at[pl.ds(1, 2)], sems.at[5, 3]),
            pltpu.make_async_copy(bsum_in, total, sems.at[0, 4]),
        ]

    @pl.when(g == 0)
    def _():
        for copy in small + cots:
            copy.start()

    Loader(ext, sems, place, [x_ref], sides, ends, w_ref, w_buf).step(g)

    @pl.when(g == 0)
    def _():
        for copy in small + cots[:1]:
            copy.wait()
        if not outer:
            total[...] = jnp.zeros_like(total)
            acc[...] = jnp.zeros_like(acc)

    pl.when(g == 1)(lambda: cots[1].wait())
    put_rows(cot, cot_buf[g].astype(f32))
    bias = b_buf[:, :1].astype(f32)

    def pair(k, carry):
        a = 2 * k
        cols = jnp.concatenate([window(ext, r, a), window(ext, r, a + 1)], axis=1)
        both = jnp.dot(w_buf[...], cols, preferred_element_type=f32)
        rows = []
        for s in range(2):
            pre = taps_sum(both[:, s * z : (s + 1) * z]) + bias
            d = forward_column(pre, cot, res, a + s, na)
            delta_ref[0, a + s] = d
            total[...] += d.astype(f32)
            rows.append(d)
        if not outer:
            rows = jnp.concatenate([shifted(d) for d in rows], axis=1)
            acc[...] += lax.dot_general(rows, cols, (((1,), (1,)), ((), ())),
                                        preferred_element_type=f32)
        return carry

    lax.fori_loop(0, na // 2, pair, 0)
    out_ref[0, :, 0] = get_rows(res, c, na).astype(bf16)
    slot = r if outer else g
    near_ref[slot] = delta_ref[0, (na - 1) * (1 - p)]
    far_ref[slot] = delta_ref[0, (na - 1) * p]
    if outer:
        @pl.when(g != q)
        def _():
            near_row[...] = delta_ref[0]

        @pl.when(g == q)
        def _():
            far_row[...] = delta_ref[0]


def forward(place, x, sides, ends, w, b, cot, before=None):
    _, na, c, z = x.shape
    outer = before is not None
    field = pl.BlockSpec(
        (1, c, 1, na, z), lambda g, _: (0, 0, 3 * g if outer else 1 + g, 0, 0))
    args = [x, *sides, *ends, w, b, cot]
    face, row = shape((4 if outer else 2, c, z)), shape((na, c, z))
    rest = [face, face, shape((c, z), f32)]
    rest += [row, row] if outer else [shape((3 * c, K9), f32)]
    alias = None
    if outer:
        alias = {1 + len(args): 0}
        args += before
    return call(
        lambda *refs: forward_body(outer, *refs), place, 2,
        args, [ANY] * len(args), [shape(cot.shape), shape((2, na, c, z))] + rest,
        [field, pl.BlockSpec((1, na, c, z), lambda g, _: (g, 0, 0, 0))]
        + [full(y) for y in rest],
        ext_scratch(na, c, z) + [pltpu.VMEM((z // 128, c * na, 128), f32)] * 2
        + [pltpu.VMEM((2, c, na, z), bf16), pltpu.VMEM(b.shape, bf16)],
        5000000000, alias)


def weight_body(place, x_ref, *refs):
    sides, ends = refs[:2], refs[2:4]
    (d_in, bsum_in, acc_in, keep_ref, send_ref,
     ext, sems, acc, flat, d_ref, bsum_ref) = refs[4:]
    g = pl.program_id(0)
    r = 3 * g
    p = place[0]
    _, na, c, _ = x_ref.shape
    deltas = [pltpu.make_async_copy(d_in.at[k], d_ref.at[k], sems.at[1 + k, 3])
              for k in range(2)]
    sums = pltpu.make_async_copy(bsum_in, bsum_ref, sems.at[3, 3])
    pl.when(g == 0)(lambda: deltas[0].start())
    Loader(ext, sems, place, [x_ref], sides, ends, acc_in, acc).step(g)

    @pl.when(g == 0)
    def _():
        deltas[1].start()
        sums.start()
        deltas[0].wait()

    @pl.when(g == 1)
    def _():
        deltas[1].wait()
        sums.wait()

    def pair(k, carry):
        a = 2 * k
        cols = jnp.concatenate([window(ext, r, a), window(ext, r, a + 1)], axis=1)
        rows = jnp.concatenate([shifted(d_ref[g, a]), shifted(d_ref[g, a + 1])], axis=1)
        acc[...] += lax.dot_general(rows, cols, (((1,), (1,)), ((), ())),
                                    preferred_element_type=f32)
        return carry

    lax.fori_loop(0, na // 2, pair, 0)

    def tiles(low, high):
        for s in range(4):
            first = 24 * ((place[2] + s) % 4)
            for b in range(3):
                rows = pl.ds(pl.multiple_of(first + 8 * b, 8), 8)
                for l in range(21):
                    n = b * 21 + l
                    (low if n < 32 else high)[s, n % 32] = (
                        flat[rows, 128 * l : 128 * l + 128] * inverse_scale
                    ).astype(bf16)
            high[s, 31] = jnp.zeros((8, 128), bf16)

    @pl.when(g == 1)
    def _():
        flat[:, 27 * c :] = jnp.zeros((c, flat.shape[1] - 27 * c), f32)
        for ij in range(9):
            for k in range(3):
                t = 3 * ij + k
                flat[:, t * c : (t + 1) * c] = acc[k * c : (k + 1) * c, ij * c : (ij + 1) * c]
        flat[:, 27 * c : 27 * c + 1] = jnp.sum(bsum_ref[...], axis=1, keepdims=True)
        pl.when(p == 0)(lambda: tiles(keep_ref, send_ref))
        pl.when(p == 1)(lambda: tiles(send_ref, keep_ref))


def weight_terms(place, x, sides, ends, d_out, bsum, acc):
    _, na, c, z = x.shape
    half = shape((4, 32, 8, 128))
    return call(
        weight_body, place, 2, [x, *sides, *ends, d_out, bsum, acc],
        [ANY] * 8,
        [half, half], [full(half), full(half)],
        ext_scratch(na, c, z)[:2] + [pltpu.VMEM((3 * c, K9), f32),
                                     pltpu.VMEM((c, 21 * 128), f32),
                                     pltpu.VMEM(d_out.shape, bf16),
                                     pltpu.VMEM(bsum.shape, f32)],
        2500000000)


def backward_body(place, d_in, d_out, *refs):
    sides, ends = refs[:2], refs[2:4]
    w_ref, out_ref, ext, sems, w_buf, res = refs[4:]
    r = pl.program_id(0)
    _, na, c, z = d_in.shape
    Loader(ext, sems, place, [d_in, d_out], sides, ends, w_ref, w_buf).each(r)

    def pair(k, carry):
        a = 2 * k
        cols = jnp.concatenate([window(ext, r, a), window(ext, r, a + 1)], axis=1)
        both = jnp.dot(w_buf[...], cols, preferred_element_type=f32)
        for s in range(2):
            put_column(res, a + s, na, taps_sum(both[:, s * z : (s + 1) * z]))
        return carry

    lax.fori_loop(0, na // 2, pair, 0)
    out_ref[0, :, 0] = get_rows(res, c, na).astype(bf16)


def backward(place, d_in, d_out, sides, ends, w):
    _, na, c, z = d_in.shape
    args = [d_in, d_out, *sides, *ends, w]
    return call(
        backward_body, place, 4, args, [ANY] * len(args), shape((1, c, 4, na, z)),
        pl.BlockSpec((1, c, 1, na, z), lambda r, _: (0, 0, r, 0, 0)),
        ext_scratch(na, c, z) + [pltpu.VMEM((z // 128, c * na, 128), f32)], 5000000000)


def near_pairs(axis):
    return [(i, i ^ 1) for i in range(lax.axis_size(axis))]


def far_pairs(axis):
    n = lax.axis_size(axis)
    pairs = [(i, i - 1 if i % 2 == 0 else i + 1) for i in range(n)]
    if axis == "azi":
        return [(i, j % n) for i, j in pairs]
    return [(i, j) for i, j in pairs if 0 <= j < n]


def swap(x, axis):
    near, far = x
    got_far = lax.ppermute(far, axis, far_pairs(axis))
    got_near = lax.ppermute(near, axis, near_pairs(axis))
    return got_near, got_far


def sum_over(x, axis, step):
    n = lax.axis_size(axis)
    parts = [x] + [
        lax.ppermute(x, axis, [(i, (i + step * s) % n) for i in range(n)]) for s in (1, 2, 3)
    ]
    a, b, c, d = (y.astype(f32) for y in parts)
    return (a + c) + (b + d)


def reduce_terms(keep, send):
    core = [(i, i ^ 1) for i in range(lax.axis_size("azi"))]
    got = lax.ppermute(send, "azi", core)
    mine = [keep[s].astype(f32) + got[s].astype(f32) for s in range(4)]
    total = mine[0]
    for s in (1, 2, 3):
        y = lax.ppermute(mine[s].astype(bf16), "dp", [(i, (i + s) % 4) for i in range(4)])
        total = total + y.astype(f32)
    n = lax.axis_size("rad")
    for step in (2, 4):
        total = total.astype(bf16)
        y = lax.ppermute(total, "rad", [(i, i ^ step) for i in range(n)])
        total = total.astype(f32) + y.astype(f32)
    total = sum_over(total.astype(bf16), "azi", 2).astype(bf16)
    y = lax.ppermute(total, "rad", [(i, i ^ 1) for i in range(lax.axis_size("rad"))])
    total = total.astype(f32) + y.astype(f32)
    y = lax.ppermute(total, "azi", core)
    low = lax.axis_index("azi") % 2 == 0
    return jnp.concatenate([jnp.where(low, total, y), jnp.where(low, y, total)], axis=0)


def whole_weights(weight, bias):
    rows, width = weight.shape
    packed = jnp.concatenate([weight, jnp.broadcast_to(bias[:, None], (rows, 128))], axis=1)
    pieces = [packed] + [
        lax.ppermute(packed, "dp", [(i, (i + s) % 4) for i in range(4)]) for s in (1, 2, 3)
    ]
    order = (lax.axis_index("dp") - jnp.arange(4)) % 4
    whole = jnp.stack(pieces)[order].reshape(4 * rows, packed.shape[1])
    taps = whole[:, :width].reshape(4 * rows, 3, 3, 3, C)
    w_fwd = taps.transpose(3, 0, 1, 2, 4).reshape(3 * C, K9)
    w_back = taps[:, ::-1, ::-1, ::-1].transpose(3, 4, 1, 2, 0).reshape(3 * C, K9)
    return w_fwd, w_back, whole[:, width : width + 128]


def on_device(inputs, weight, bias, cotangent):
    place = jnp.stack(
        [lax.axis_index("azi") % 2, lax.axis_index("rad") % 2, lax.axis_index("dp")]
    ).astype(jnp.int32)
    x, near_face, far_face = to_columns(place, inputs)
    sides = swap((near_face, far_face), "azi")
    ends = swap(edges(place, x, *sides), "rad")
    w_fwd, w_back, b_col = whole_weights(weight, bias)
    out, d_in, near_in, far_in, bsum, acc = forward(
        place, x, sides, (), w_fwd, b_col, cotangent)
    output, d_out, near_face, far_face, bsum, d_near, d_far = forward(
        place, x, sides, ends, w_fwd, b_col, cotangent, [out, near_in, far_in, bsum])
    d_ends = swap((d_near, d_far), "rad")
    keep, send = weight_terms(place, x, sides, ends, d_out, bsum, acc)
    d_sides = swap(six_rows(place, near_face, far_face, d_ends), "azi")
    tiles = reduce_terms(keep, send)
    input_grad = backward(place, d_in, d_out, d_sides, d_ends, w_back)
    summed = tiles[:63].reshape(3, 21, 8, 128).transpose(0, 2, 1, 3).reshape(24, 21 * 128)
    return output, input_grad, summed[:, : 27 * C], summed[:, 27 * C]


def solution(mesh):
    return jax.shard_map(
        on_device,
        mesh=mesh,
        in_specs=(
            P("dp", None, "rad", "azi", None),
            P("dp", None),
            P("dp"),
            P("dp", None, "rad", "azi", None),
        ),
        out_specs=(
            P("dp", None, "rad", "azi", None),
            P("dp", None, "rad", "azi", None),
            P("dp", None),
            P("dp"),
        ),
        check_vma=False,
    )
```

```python
import jax
import jax.numpy as jnp
from jax import lax
from jax.experimental import pallas as pl
from jax.experimental.pallas import tpu as pltpu
from jax.sharding import PartitionSpec as P


inverse_scale = 1.0 / 1024.0
bf16 = jnp.bfloat16
f32 = jnp.float32
C = 96
K9 = 9 * C


def full(x):
    return pl.BlockSpec(x.shape, lambda *_: (0,) * len(x.shape))


def shape(dims, dtype=bf16):
    return jax.ShapeDtypeStruct(dims, dtype)


def call(body, place, grid, args, in_specs, outs, out_specs, scratch, cost, alias=None):
    return pl.pallas_call(
        body,
        grid_spec=pltpu.PrefetchScalarGridSpec(
            num_scalar_prefetch=1, grid=(grid,), in_specs=in_specs, out_specs=out_specs,
            scratch_shapes=scratch),
        out_shape=outs,
        input_output_aliases=alias or {},
        compiler_params=pltpu.CompilerParams(
            dimension_semantics=("arbitrary",), vmem_limit_bytes=56 * 1024 * 1024),
        cost_estimate=pl.CostEstimate(flops=cost, transcendentals=0, bytes_accessed=4000000),
    )(place, *args)


def put_rows(tmp, cells):
    c, na, z = cells.shape
    flat = cells.reshape(c * na, z)
    for h in range(z // 128):
        tmp[h] = flat[:, 128 * h : 128 * h + 128]


def get_rows(tmp, c, na):
    flat = jnp.concatenate([tmp[h] for h in range(tmp.shape[0])], axis=1)
    return flat.reshape(c, na, flat.shape[1])


def get_column(tmp, a, c, na):
    return jnp.concatenate(
        [tmp[h, pl.ds(a, c, stride=na), :] for h in range(tmp.shape[0])], axis=1
    )


def put_column(tmp, a, na, column):
    c = column.shape[0]
    for h in range(tmp.shape[0]):
        tmp[h, pl.ds(a, c, stride=na), :] = column[:, 128 * h : 128 * h + 128]


def columns_body(place, x_ref, o_ref, near_ref, far_ref, near_row, far_row, tmp):
    c, nr, na = x_ref.shape[1:4]
    p, q = place[0], place[1]
    for r in range(nr):
        put_rows(tmp, x_ref[0, :, r].astype(f32))
        for a in range(na):
            o_ref[r, a] = get_column(tmp, a, c, na).astype(bf16)
        near_ref[r] = o_ref[r, (na - 1) * (1 - p)]
        far_ref[r] = o_ref[r, (na - 1) * p]
    near_row[1 : na + 1] = o_ref[(nr - 1) * (1 - q)]
    far_row[1 : na + 1] = o_ref[(nr - 1) * q]


def to_columns(place, field):
    _, c, nr, na, nz = field.shape
    face, row = shape((nr, c, nz)), shape((na + 2, c, nz))
    part = c // 2
    rest = [face, face, row, row]
    return call(
        columns_body, place, 2, (field,),
        [pl.BlockSpec((1, part, nr, na, nz), lambda g, _: (0, g, 0, 0, 0))],
        [shape((nr, na, c, nz))] + rest,
        [pl.BlockSpec((nr, na, part, nz), lambda g, _: (0, 0, g, 0))]
        + [pl.BlockSpec((y.shape[0], part, nz), lambda g, _: (0, g, 0)) for y in rest],
        [pltpu.VMEM((nz // 128, part * na, 128), f32)], 10000000)


ANY = pl.BlockSpec(memory_space=pl.ANY)


def insert_body(axis, place, a_near, a_far, h_near, h_far, out_near, out_far, buf, sems):
    along, across = place[axis], place[1 - axis]
    last = h_near.shape[0] - 1
    end = out_near.shape[0] - 1
    loads, stores = [], []
    for k, (out, at) in enumerate(
        ((out_near, last * (1 - across)), (out_far, last * across))
    ):
        for n, (halo, to) in enumerate(((h_near, end * (1 - along)), (h_far, end * along))):
            i = 2 * k + n
            loads.append(pltpu.make_async_copy(halo.at[at], buf.at[i], sems.at[0, i]))
            stores.append(pltpu.make_async_copy(buf.at[i], out.at[to], sems.at[1, i]))
    for copy in loads:
        copy.start()
    for load, store in zip(loads, stores):
        load.wait()
        store.start()
    for copy in stores:
        copy.wait()


def insert(place, axis, messages, halos):
    near, far = messages
    _, c, z = near.shape
    return call(
        lambda *refs: insert_body(axis, *refs), place, 1, (near, far, *halos), [ANY] * 4,
        [shape(near.shape)] * 2, [ANY, ANY],
        [pltpu.VMEM((4, c, z), bf16), pltpu.SemaphoreType.DMA((2, 4))], 1000000, {1: 0, 2: 1})


class Loader:
    def __init__(self, ext, sems, place, rows, sides, ends, w, w_buf):
        p, q = place[0], place[1]
        self.w = pltpu.make_async_copy(w, w_buf, sems.at[0, 3])
        self.ext, self.sems, self.ends = ext, sems, ends
        na = ext.shape[1] - 2
        six = sides[0].shape[0] == 6
        self.own = {}
        for e in range(6):
            copies = []
            if e in (0, 5):
                if not ends:
                    continue
            elif len(rows) == 1:
                copies.append(pltpu.make_async_copy(
                    rows[0].at[e - 1], ext.at[e, pl.ds(1, na)], sems.at[e, 0]))
            else:
                row = rows[0].at[e - 2] if e in (2, 3) else rows[1].at[0 if e == 1 else 1]
                copies.append(pltpu.make_async_copy(row, ext.at[e, pl.ds(1, na)], sems.at[e, 0]))
            if six or e not in (0, 5):
                for k, col in enumerate(((na + 1) * (1 - p), (na + 1) * p)):
                    copies.append(pltpu.make_async_copy(
                        sides[k].at[e if six else e - 1], ext.at[e, col], sems.at[e, 1 + k]))
            self.own[e] = copies
        self.q = q

    def end(self, k, e):
        dst = self.ext.at[e]
        if self.ends[k].shape[0] < self.ext.shape[1]:
            dst = self.ext.at[e, pl.ds(1, self.ends[k].shape[0])]
        return pltpu.make_async_copy(self.ends[k], dst, self.sems.at[e, 0])

    def start(self):
        for e in (1, 2):
            for copy in self.own[e]:
                copy.start()
        if self.ends:
            self.end(0, 5 * (1 - self.q)).start()
            self.end(1, 5 * self.q).start()
        self.w.start()
        for e in (0, 5, 3, 4):
            for copy in self.own.get(e, ()):
                copy.start()

    def wait(self, *rows):
        for e in rows:
            if e in (0, 5):
                self.end(0, e).wait()
            for copy in self.own[e]:
                copy.wait()

    def step(self, g):
        first, second = ((0, 1, 2), (3, 4, 5)) if self.ends else ((1, 2, 3), (4,))

        @pl.when(g == 0)
        def _():
            self.start()
            self.wait(*first)
            self.w.wait()

        pl.when(g == 1)(lambda: self.wait(*second))

    def each(self, r):
        @pl.when(r == 0)
        def _():
            self.start()
            self.wait(0, 1, 2)
            self.w.wait()

        for k in (1, 2, 3):
            pl.when(r == k)(lambda k=k: self.wait(k + 2))


def ext_scratch(na, c, z):
    return [pltpu.VMEM((6, na + 2, c, z), bf16), pltpu.SemaphoreType.DMA((6, 5)),
            pltpu.VMEM((3 * c, K9), bf16)]


def window(ext, r, a):
    c, z = ext.shape[2], ext.shape[3]
    return jnp.concatenate(
        [ext[r + i, pl.ds(a, 3)].reshape(3 * c, z) for i in range(3)], axis=0
    )


def taps_sum(parts):
    c = parts.shape[0] // 3
    z = parts.shape[1]
    lane = lax.broadcasted_iota(jnp.int32, (c, z), 1)
    before = jnp.where(lane == 0, 0.0, pltpu.roll(parts[:c], 1, 1))
    after = jnp.where(lane == z - 1, 0.0, pltpu.roll(parts[2 * c :], z - 1, 1))
    return parts[c : 2 * c] + before + after


def forward_column(pre, cot, res, a, na):
    gate = jax.nn.sigmoid(pre)
    put_column(res, a, na, pre * gate)
    d = get_column(cot, a, pre.shape[0], na) * gate * (1.0 + pre * (1.0 - gate))
    return d.astype(bf16)


def shifted(d):
    c, z = d.shape
    lane = lax.broadcasted_iota(jnp.int32, (c, z), 1)
    d = d.astype(f32)
    ahead = jnp.where(lane == z - 1, 0.0, pltpu.roll(d, z - 1, 1))
    behind = jnp.where(lane == 0, 0.0, pltpu.roll(d, 1, 1))
    return jnp.concatenate([ahead, d, behind], axis=0).astype(bf16)


def forward_body(outer, place, x_ref, *refs):
    sides, refs = refs[:2], refs[2:]
    ends = ()
    if outer:
        ends, refs = refs[:2], refs[2:]
    w_ref, b_ref, cot_ref, *refs = refs
    if outer:
        _, near_in, far_in, bsum_in, *refs = refs
        (out_ref, delta_ref, near_ref, far_ref, total, near_row, far_row,
         ext, sems, w_buf, cot, res, cot_buf, b_buf) = refs
    else:
        (out_ref, delta_ref, near_ref, far_ref, total, acc,
         ext, sems, w_buf, cot, res, cot_buf, b_buf) = refs
    g = pl.program_id(0)
    r = 3 * g if outer else 1 + g
    p, q = place[0], place[1]
    _, na, c, z = x_ref.shape
    cots = [
        pltpu.make_async_copy(cot_ref.at[0, :, 3 * k if outer else 1 + k], cot_buf.at[k],
                              sems.at[1 + k, 3])
        for k in range(2)
    ]
    small = [pltpu.make_async_copy(b_ref, b_buf, sems.at[3, 3])]
    if outer:
        small += [
            pltpu.make_async_copy(near_in, near_ref.at[pl.ds(2, 2)], sems.at[4, 3]),
            pltpu.make_async_copy(far_in, far_ref.at[pl.ds(2, 2)], sems.at[5, 3]),
            pltpu.make_async_copy(bsum_in, total, sems.at[0, 4]),
        ]

    @pl.when(g == 0)
    def _():
        for copy in small + cots:
            copy.start()

    Loader(ext, sems, place, [x_ref], sides, ends, w_ref, w_buf).step(g)

    @pl.when(g == 0)
    def _():
        for copy in small + cots[:1]:
            copy.wait()
        if not outer:
            total[...] = jnp.zeros_like(total)
            acc[...] = jnp.zeros_like(acc)

    pl.when(g == 1)(lambda: cots[1].wait())
    put_rows(cot, cot_buf[g].astype(f32))
    bias = b_buf[:, :1].astype(f32)

    def pair(k, carry):
        a = 2 * k
        cols = jnp.concatenate([window(ext, r, a), window(ext, r, a + 1)], axis=1)
        both = jnp.dot(w_buf[...], cols, preferred_element_type=f32)
        rows = []
        for s in range(2):
            pre = taps_sum(both[:, s * z : (s + 1) * z]) + bias
            d = forward_column(pre, cot, res, a + s, na)
            delta_ref[0, a + s] = d
            total[...] += d.astype(f32)
            rows.append(d)
        if not outer:
            rows = jnp.concatenate([shifted(d) for d in rows], axis=1)
            acc[...] += lax.dot_general(rows, cols, (((1,), (1,)), ((), ())),
                                        preferred_element_type=f32)
        return carry

    lax.fori_loop(0, na // 2, pair, 0)
    out_ref[0, :, 0] = get_rows(res, c, na).astype(bf16)
    slot = r + 1 if outer else g
    near_ref[slot] = delta_ref[0, (na - 1) * (1 - p)]
    far_ref[slot] = delta_ref[0, (na - 1) * p]
    if outer:
        @pl.when(g != q)
        def _():
            near_row[...] = delta_ref[0]

        @pl.when(g == q)
        def _():
            far_row[...] = delta_ref[0]


def forward(place, x, sides, ends, w, b, cot, before=None):
    _, na, c, z = x.shape
    outer = before is not None
    field = pl.BlockSpec(
        (1, c, 1, na, z), lambda g, _: (0, 0, 3 * g if outer else 1 + g, 0, 0))
    args = [x, *sides, *ends, w, b, cot]
    face, row = shape((6 if outer else 2, c, z)), shape((na, c, z))
    rest = [face, face, shape((c, z), f32)]
    rest += [row, row] if outer else [shape((3 * c, K9), f32)]
    alias = None
    if outer:
        alias = {1 + len(args): 0}
        args += before
    return call(
        lambda *refs: forward_body(outer, *refs), place, 2,
        args, [ANY] * len(args), [shape(cot.shape), shape((2, na, c, z))] + rest,
        [field, pl.BlockSpec((1, na, c, z), lambda g, _: (g, 0, 0, 0))]
        + [full(y) for y in rest],
        ext_scratch(na, c, z) + [pltpu.VMEM((z // 128, c * na, 128), f32)] * 2
        + [pltpu.VMEM((2, c, na, z), bf16), pltpu.VMEM(b.shape, bf16)],
        5000000000, alias)


def weight_body(place, x_ref, *refs):
    sides, ends = refs[:2], refs[2:4]
    (d_in, bsum_in, acc_in, keep_ref, send_ref,
     ext, sems, acc, flat, d_ref, bsum_ref) = refs[4:]
    g = pl.program_id(0)
    r = 3 * g
    p = place[0]
    _, na, c, _ = x_ref.shape
    deltas = [pltpu.make_async_copy(d_in.at[k], d_ref.at[k], sems.at[1 + k, 3])
              for k in range(2)]
    sums = pltpu.make_async_copy(bsum_in, bsum_ref, sems.at[3, 3])
    pl.when(g == 0)(lambda: deltas[0].start())
    Loader(ext, sems, place, [x_ref], sides, ends, acc_in, acc).step(g)

    @pl.when(g == 0)
    def _():
        deltas[1].start()
        sums.start()
        deltas[0].wait()

    @pl.when(g == 1)
    def _():
        deltas[1].wait()
        sums.wait()

    def pair(k, carry):
        a = 2 * k
        cols = jnp.concatenate([window(ext, r, a), window(ext, r, a + 1)], axis=1)
        rows = jnp.concatenate([shifted(d_ref[g, a]), shifted(d_ref[g, a + 1])], axis=1)
        acc[...] += lax.dot_general(rows, cols, (((1,), (1,)), ((), ())),
                                    preferred_element_type=f32)
        return carry

    lax.fori_loop(0, na // 2, pair, 0)

    def tiles(low, high):
        for s in range(4):
            first = 24 * ((place[2] + s) % 4)
            for b in range(3):
                rows = pl.ds(pl.multiple_of(first + 8 * b, 8), 8)
                for l in range(21):
                    n = b * 21 + l
                    (low if n < 32 else high)[s, n % 32] = (
                        flat[rows, 128 * l : 128 * l + 128] * inverse_scale
                    ).astype(bf16)
            high[s, 31] = jnp.zeros((8, 128), bf16)

    @pl.when(g == 1)
    def _():
        flat[:, 27 * c :] = jnp.zeros((c, flat.shape[1] - 27 * c), f32)
        for ij in range(9):
            for k in range(3):
                t = 3 * ij + k
                flat[:, t * c : (t + 1) * c] = acc[k * c : (k + 1) * c, ij * c : (ij + 1) * c]
        flat[:, 27 * c : 27 * c + 1] = jnp.sum(bsum_ref[...], axis=1, keepdims=True)
        pl.when(p == 0)(lambda: tiles(keep_ref, send_ref))
        pl.when(p == 1)(lambda: tiles(send_ref, keep_ref))


def weight_terms(place, x, sides, ends, d_out, bsum, acc):
    _, na, c, z = x.shape
    half = shape((4, 32, 8, 128))
    return call(
        weight_body, place, 2, [x, *sides, *ends, d_out, bsum, acc],
        [ANY] * 8,
        [half, half], [full(half), full(half)],
        ext_scratch(na, c, z)[:2] + [pltpu.VMEM((3 * c, K9), f32),
                                     pltpu.VMEM((c, 21 * 128), f32),
                                     pltpu.VMEM(d_out.shape, bf16),
                                     pltpu.VMEM(bsum.shape, f32)],
        2500000000)


def backward_body(place, d_in, d_out, *refs):
    sides, ends = refs[:2], refs[2:4]
    w_ref, out_ref, ext, sems, w_buf, res = refs[4:]
    r = pl.program_id(0)
    _, na, c, z = d_in.shape
    Loader(ext, sems, place, [d_in, d_out], sides, ends, w_ref, w_buf).each(r)

    def pair(k, carry):
        a = 2 * k
        cols = jnp.concatenate([window(ext, r, a), window(ext, r, a + 1)], axis=1)
        both = jnp.dot(w_buf[...], cols, preferred_element_type=f32)
        for s in range(2):
            put_column(res, a + s, na, taps_sum(both[:, s * z : (s + 1) * z]))
        return carry

    lax.fori_loop(0, na // 2, pair, 0)
    out_ref[0, :, 0] = get_rows(res, c, na).astype(bf16)


def backward(place, d_in, d_out, sides, ends, w):
    _, na, c, z = d_in.shape
    args = [d_in, d_out, *sides, *ends, w]
    return call(
        backward_body, place, 4, args, [ANY] * len(args), shape((1, c, 4, na, z)),
        pl.BlockSpec((1, c, 1, na, z), lambda r, _: (0, 0, r, 0, 0)),
        ext_scratch(na, c, z) + [pltpu.VMEM((z // 128, c * na, 128), f32)], 5000000000)


def near_pairs(axis):
    return [(i, i ^ 1) for i in range(lax.axis_size(axis))]


def far_pairs(axis):
    n = lax.axis_size(axis)
    pairs = [(i, i - 1 if i % 2 == 0 else i + 1) for i in range(n)]
    if axis == "azi":
        return [(i, j % n) for i, j in pairs]
    return [(i, j) for i, j in pairs if 0 <= j < n]


def swap(x, axis):
    near, far = x
    got_far = lax.ppermute(far, axis, far_pairs(axis))
    got_near = lax.ppermute(near, axis, near_pairs(axis))
    return got_near, got_far


def sum_over(x, axis, step):
    n = lax.axis_size(axis)
    parts = [x] + [
        lax.ppermute(x, axis, [(i, (i + step * s) % n) for i in range(n)]) for s in (1, 2, 3)
    ]
    a, b, c, d = (y.astype(f32) for y in parts)
    return (a + c) + (b + d)


def reduce_terms(keep, send):
    core = [(i, i ^ 1) for i in range(lax.axis_size("azi"))]
    got = lax.ppermute(send, "azi", core)
    mine = [keep[s].astype(f32) + got[s].astype(f32) for s in range(4)]
    total = mine[0]
    for s in (1, 2, 3):
        y = lax.ppermute(mine[s].astype(bf16), "dp", [(i, (i + s) % 4) for i in range(4)])
        total = total + y.astype(f32)
    n = lax.axis_size("rad")
    total = total.astype(bf16)
    y = lax.ppermute(total, "rad", [(i, i ^ 2) for i in range(n)])
    total = (total.astype(f32) + y.astype(f32)).astype(bf16)
    a, b, c = (
        lax.ppermute(total, "rad", [(i, i ^ step) for i in range(n)]) for step in (1, 4, 5)
    )
    a, b, c, d = (y.astype(f32) for y in (a, b, c, total))
    total = (d + a) + (b + c)
    total = sum_over(total.astype(bf16), "azi", 2)
    y = lax.ppermute(total, "azi", core)
    low = lax.axis_index("azi") % 2 == 0
    return jnp.concatenate([jnp.where(low, total, y), jnp.where(low, y, total)], axis=0)


def whole_weights(weight, bias):
    rows, width = weight.shape
    packed = jnp.concatenate([weight, jnp.broadcast_to(bias[:, None], (rows, 128))], axis=1)
    pieces = [packed] + [
        lax.ppermute(packed, "dp", [(i, (i + s) % 4) for i in range(4)]) for s in (1, 2, 3)
    ]
    order = (lax.axis_index("dp") - jnp.arange(4)) % 4
    whole = jnp.stack(pieces)[order].reshape(4 * rows, packed.shape[1])
    taps = whole[:, :width].reshape(4 * rows, 3, 3, 3, C)
    w_fwd = taps.transpose(3, 0, 1, 2, 4).reshape(3 * C, K9)
    w_back = taps[:, ::-1, ::-1, ::-1].transpose(3, 4, 1, 2, 0).reshape(3 * C, K9)
    return w_fwd, w_back, whole[:, width : width + 128]


def on_device(inputs, weight, bias, cotangent):
    place = jnp.stack(
        [lax.axis_index("azi") % 2, lax.axis_index("rad") % 2, lax.axis_index("dp")]
    ).astype(jnp.int32)
    x, near_face, far_face, near_row, far_row = to_columns(place, inputs)
    sides = swap((near_face, far_face), "azi")
    ends = swap(insert(place, 0, (near_row, far_row), sides), "rad")
    w_fwd, w_back, b_col = whole_weights(weight, bias)
    out, d_in, near_in, far_in, bsum, acc = forward(
        place, x, sides, (), w_fwd, b_col, cotangent)
    output, d_out, near_face, far_face, bsum, d_near, d_far = forward(
        place, x, sides, ends, w_fwd, b_col, cotangent, [out, near_in, far_in, bsum])
    d_ends = swap((d_near, d_far), "rad")
    keep, send = weight_terms(place, x, sides, ends, d_out, bsum, acc)
    d_sides = swap(insert(place, 1, (near_face, far_face), d_ends), "azi")
    tiles = reduce_terms(keep, send)
    input_grad = backward(place, d_in, d_out, d_sides, d_ends, w_back)
    summed = tiles[:63].reshape(3, 21, 8, 128).transpose(0, 2, 1, 3).reshape(24, 21 * 128)
    return output, input_grad, summed[:, : 27 * C], summed[:, 27 * C]


def solution(mesh):
    return jax.shard_map(
        on_device,
        mesh=mesh,
        in_specs=(
            P("dp", None, "rad", "azi", None),
            P("dp", None),
            P("dp"),
            P("dp", None, "rad", "azi", None),
        ),
        out_specs=(
            P("dp", None, "rad", "azi", None),
            P("dp", None, "rad", "azi", None),
            P("dp", None),
            P("dp"),
        ),
        check_vma=False,
    )
```

```python
import jax
import jax.numpy as jnp
from jax import lax
from jax.experimental import pallas as pl
from jax.experimental.pallas import tpu as pltpu
from jax.sharding import PartitionSpec as P


inverse_scale = 1.0 / 1024.0
bf16 = jnp.bfloat16
f32 = jnp.float32
C = 96
K9 = 9 * C


def full(x):
    return pl.BlockSpec(x.shape, lambda *_: (0,) * len(x.shape))


def shape(dims, dtype=bf16):
    return jax.ShapeDtypeStruct(dims, dtype)


def call(body, grid, args, in_specs, outs, out_specs, scratch, cost, alias=None):
    def placed(*refs):
        place = (lax.axis_index("azi") & 1, lax.axis_index("rad") & 1, lax.axis_index("dp"))
        body(place, *refs)

    return pl.pallas_call(
        placed,
        grid_spec=pl.GridSpec(grid=(grid,), in_specs=in_specs, out_specs=out_specs,
                              scratch_shapes=scratch),
        out_shape=outs,
        input_output_aliases=alias or {},
        compiler_params=pltpu.CompilerParams(
            dimension_semantics=("arbitrary",), vmem_limit_bytes=56 * 1024 * 1024),
        cost_estimate=pl.CostEstimate(flops=cost, transcendentals=0, bytes_accessed=4000000),
    )(*args)


def put_rows(tmp, cells):
    c, na, z = cells.shape
    flat = cells.reshape(c * na, z)
    for h in range(z // 128):
        tmp[h] = flat[:, 128 * h : 128 * h + 128]


def get_rows(tmp, c, na):
    flat = jnp.concatenate([tmp[h] for h in range(tmp.shape[0])], axis=1)
    return flat.reshape(c, na, flat.shape[1])


def get_column(tmp, a, c, na):
    return jnp.concatenate(
        [tmp[h, pl.ds(a, c, stride=na), :] for h in range(tmp.shape[0])], axis=1
    )


def put_column(tmp, a, na, column):
    c = column.shape[0]
    for h in range(tmp.shape[0]):
        tmp[h, pl.ds(a, c, stride=na), :] = column[:, 128 * h : 128 * h + 128]


def columns_body(place, x_ref, o_ref, near_ref, far_ref, near_row, far_row, tmp):
    c, nr, na = x_ref.shape[1:4]
    p, q = place[0], place[1]
    for r in range(nr):
        put_rows(tmp, x_ref[0, :, r].astype(f32))
        for a in range(na):
            o_ref[r, a] = get_column(tmp, a, c, na).astype(bf16)
        near_ref[r] = o_ref[r, (na - 1) * (1 - p)]
        far_ref[r] = o_ref[r, (na - 1) * p]
    near_row[1 : na + 1] = o_ref[(nr - 1) * (1 - q)]
    far_row[1 : na + 1] = o_ref[(nr - 1) * q]


def to_columns(field):
    _, c, nr, na, nz = field.shape
    face, row = shape((nr, c, nz)), shape((na + 2, c, nz))
    part = c // 2
    rest = [face, face, row, row]
    return call(
        columns_body, 2, (field,),
        [pl.BlockSpec((1, part, nr, na, nz), lambda g: (0, g, 0, 0, 0))],
        [shape((nr, na, c, nz))] + rest,
        [pl.BlockSpec((nr, na, part, nz), lambda g: (0, 0, g, 0))]
        + [pl.BlockSpec((y.shape[0], part, nz), lambda g: (0, g, 0)) for y in rest],
        [pltpu.VMEM((nz // 128, part * na, 128), f32)], 10000000)


ANY = pl.BlockSpec(memory_space=pl.ANY)


def insert_body(axis, place, a_near, a_far, h_near, h_far, out_near, out_far, buf, sems):
    along, across = place[axis], place[1 - axis]
    last = h_near.shape[0] - 1
    end = out_near.shape[0] - 1
    loads, stores = [], []
    for k, (out, at) in enumerate(
        ((out_near, last * (1 - across)), (out_far, last * across))
    ):
        for n, (halo, to) in enumerate(((h_near, end * (1 - along)), (h_far, end * along))):
            i = 2 * k + n
            loads.append(pltpu.make_async_copy(halo.at[at], buf.at[i], sems.at[0, i]))
            stores.append(pltpu.make_async_copy(buf.at[i], out.at[to], sems.at[1, i]))
    for copy in loads:
        copy.start()
    for load, store in zip(loads, stores):
        load.wait()
        store.start()
    for copy in stores:
        copy.wait()


def insert(axis, messages, halos):
    near, far = messages
    _, c, z = near.shape
    return call(
        lambda *refs: insert_body(axis, *refs), 1, (near, far, *halos), [ANY] * 4,
        [shape(near.shape)] * 2, [ANY, ANY],
        [pltpu.VMEM((4, c, z), bf16), pltpu.SemaphoreType.DMA((2, 4))], 1000000, {0: 0, 1: 1})


class Loader:
    def __init__(self, ext, sems, place, rows, sides, ends, w, w_buf):
        p, q = place[0], place[1]
        self.w = pltpu.make_async_copy(w, w_buf, sems.at[0, 3])
        self.ext, self.sems, self.ends = ext, sems, ends
        na = ext.shape[1] - 2
        six = sides[0].shape[0] == 6
        self.own = {}
        for e in range(6):
            copies = []
            if e in (0, 5):
                if not ends:
                    continue
            elif len(rows) == 1:
                copies.append(pltpu.make_async_copy(
                    rows[0].at[e - 1], ext.at[e, pl.ds(1, na)], sems.at[e, 0]))
            else:
                row = rows[0].at[e - 2] if e in (2, 3) else rows[1].at[0 if e == 1 else 1]
                copies.append(pltpu.make_async_copy(row, ext.at[e, pl.ds(1, na)], sems.at[e, 0]))
            if six or e not in (0, 5):
                for k, col in enumerate(((na + 1) * (1 - p), (na + 1) * p)):
                    copies.append(pltpu.make_async_copy(
                        sides[k].at[e if six else e - 1], ext.at[e, col], sems.at[e, 1 + k]))
            self.own[e] = copies
        self.q = q

    def end(self, k, e):
        dst = self.ext.at[e]
        if self.ends[k].shape[0] < self.ext.shape[1]:
            dst = self.ext.at[e, pl.ds(1, self.ends[k].shape[0])]
        return pltpu.make_async_copy(self.ends[k], dst, self.sems.at[e, 0])

    def start(self):
        for e in (1, 2):
            for copy in self.own[e]:
                copy.start()
        if self.ends:
            self.end(0, 5 * (1 - self.q)).start()
            self.end(1, 5 * self.q).start()
        self.w.start()
        for e in (0, 5, 3, 4):
            for copy in self.own.get(e, ()):
                copy.start()

    def wait(self, *rows):
        for e in rows:
            if e in (0, 5):
                self.end(0, e).wait()
            for copy in self.own[e]:
                copy.wait()

    def step(self, g):
        first, second = ((0, 1, 2), (3, 4, 5)) if self.ends else ((1, 2, 3), (4,))

        @pl.when(g == 0)
        def _():
            self.start()
            self.wait(*first)
            self.w.wait()

        pl.when(g == 1)(lambda: self.wait(*second))

    def each(self, r):
        @pl.when(r == 0)
        def _():
            self.start()
            self.wait(0, 1, 2)
            self.w.wait()

        for k in (1, 2, 3):
            pl.when(r == k)(lambda k=k: self.wait(k + 2))


def ext_scratch(na, c, z):
    return [pltpu.VMEM((6, na + 2, c, z), bf16), pltpu.SemaphoreType.DMA((6, 5)),
            pltpu.VMEM((3 * c, K9), bf16)]


def window(ext, r, a):
    c, z = ext.shape[2], ext.shape[3]
    return jnp.concatenate(
        [ext[r + i, pl.ds(a, 3)].reshape(3 * c, z) for i in range(3)], axis=0
    )


def taps_sum(parts):
    c = parts.shape[0] // 3
    z = parts.shape[1]
    lane = lax.broadcasted_iota(jnp.int32, (c, z), 1)
    before = jnp.where(lane == 0, 0.0, pltpu.roll(parts[:c], 1, 1))
    after = jnp.where(lane == z - 1, 0.0, pltpu.roll(parts[2 * c :], z - 1, 1))
    return parts[c : 2 * c] + before + after


def forward_column(pre, cot, res, a, na):
    gate = jax.nn.sigmoid(pre)
    put_column(res, a, na, pre * gate)
    d = get_column(cot, a, pre.shape[0], na) * gate * (1.0 + pre * (1.0 - gate))
    return d.astype(bf16)


def shifted(d):
    c, z = d.shape
    lane = lax.broadcasted_iota(jnp.int32, (c, z), 1)
    d = d.astype(f32)
    ahead = jnp.where(lane == z - 1, 0.0, pltpu.roll(d, z - 1, 1))
    behind = jnp.where(lane == 0, 0.0, pltpu.roll(d, 1, 1))
    return jnp.concatenate([ahead, d, behind], axis=0).astype(bf16)


def forward_body(outer, place, x_ref, *refs):
    sides, refs = refs[:2], refs[2:]
    ends = ()
    if outer:
        ends, refs = refs[:2], refs[2:]
    w_ref, b_ref, cot_ref, *refs = refs
    if outer:
        _, near_in, far_in, bsum_in, *refs = refs
        (out_ref, delta_ref, near_ref, far_ref, total, near_row, far_row,
         ext, sems, w_buf, cot, res, cot_buf, b_buf) = refs
    else:
        (out_ref, delta_ref, near_ref, far_ref, total, acc,
         ext, sems, w_buf, cot, res, cot_buf, b_buf) = refs
    g = pl.program_id(0)
    r = 3 * g if outer else 1 + g
    p, q = place[0], place[1]
    _, na, c, z = x_ref.shape
    cots = [
        pltpu.make_async_copy(cot_ref.at[0, :, 3 * k if outer else 1 + k], cot_buf.at[k],
                              sems.at[1 + k, 3])
        for k in range(2)
    ]
    small = [pltpu.make_async_copy(b_ref, b_buf, sems.at[3, 3])]
    if outer:
        small += [
            pltpu.make_async_copy(near_in, near_ref.at[pl.ds(2, 2)], sems.at[4, 3]),
            pltpu.make_async_copy(far_in, far_ref.at[pl.ds(2, 2)], sems.at[5, 3]),
            pltpu.make_async_copy(bsum_in, total, sems.at[0, 4]),
        ]

    @pl.when(g == 0)
    def _():
        for copy in small + cots:
            copy.start()

    Loader(ext, sems, place, [x_ref], sides, ends, w_ref, w_buf).step(g)

    @pl.when(g == 0)
    def _():
        for copy in small + cots[:1]:
            copy.wait()
        if not outer:
            total[...] = jnp.zeros_like(total)
            acc[...] = jnp.zeros_like(acc)

    pl.when(g == 1)(lambda: cots[1].wait())
    put_rows(cot, cot_buf[g].astype(f32))
    bias = b_buf[:, :1].astype(f32)

    def pair(k, carry):
        a = 2 * k
        cols = jnp.concatenate([window(ext, r, a), window(ext, r, a + 1)], axis=1)
        both = jnp.dot(w_buf[...], cols, preferred_element_type=f32)
        rows = []
        for s in range(2):
            pre = taps_sum(both[:, s * z : (s + 1) * z]) + bias
            d = forward_column(pre, cot, res, a + s, na)
            delta_ref[0, a + s] = d
            total[...] += d.astype(f32)
            rows.append(d)
        if not outer:
            rows = jnp.concatenate([shifted(d) for d in rows], axis=1)
            acc[...] += lax.dot_general(rows, cols, (((1,), (1,)), ((), ())),
                                        preferred_element_type=f32)
        return carry

    lax.fori_loop(0, na // 2, pair, 0)
    out_ref[0, :, 0] = get_rows(res, c, na).astype(bf16)
    slot = r + 1 if outer else g
    near_ref[slot] = delta_ref[0, (na - 1) * (1 - p)]
    far_ref[slot] = delta_ref[0, (na - 1) * p]
    if outer:
        @pl.when(g != q)
        def _():
            near_row[...] = delta_ref[0]

        @pl.when(g == q)
        def _():
            far_row[...] = delta_ref[0]


def forward(x, sides, ends, w, b, cot, before=None):
    _, na, c, z = x.shape
    outer = before is not None
    field = pl.BlockSpec(
        (1, c, 1, na, z), lambda g: (0, 0, 3 * g if outer else 1 + g, 0, 0))
    args = [x, *sides, *ends, w, b, cot]
    face, row = shape((6 if outer else 2, c, z)), shape((na, c, z))
    rest = [face, face, shape((c, z), f32)]
    rest += [row, row] if outer else [shape((3 * c, K9), f32)]
    alias = None
    if outer:
        alias = {len(args): 0}
        args += before
    return call(
        lambda *refs: forward_body(outer, *refs), 2,
        args, [ANY] * len(args), [shape(cot.shape), shape((2, na, c, z))] + rest,
        [field, pl.BlockSpec((1, na, c, z), lambda g: (g, 0, 0, 0))]
        + [full(y) for y in rest],
        ext_scratch(na, c, z) + [pltpu.VMEM((z // 128, c * na, 128), f32)] * 2
        + [pltpu.VMEM((2, c, na, z), bf16), pltpu.VMEM(b.shape, bf16)],
        5000000000, alias)


def weight_body(place, x_ref, *refs):
    sides, ends = refs[:2], refs[2:4]
    (d_in, bsum_in, acc_in, keep_ref, send_ref,
     ext, sems, acc, flat, d_ref, bsum_ref) = refs[4:]
    g = pl.program_id(0)
    r = 3 * g
    p = place[0]
    _, na, c, _ = x_ref.shape
    deltas = [pltpu.make_async_copy(d_in.at[k], d_ref.at[k], sems.at[1 + k, 3])
              for k in range(2)]
    sums = pltpu.make_async_copy(bsum_in, bsum_ref, sems.at[3, 3])
    pl.when(g == 0)(lambda: deltas[0].start())
    Loader(ext, sems, place, [x_ref], sides, ends, acc_in, acc).step(g)

    @pl.when(g == 0)
    def _():
        deltas[1].start()
        sums.start()
        deltas[0].wait()

    @pl.when(g == 1)
    def _():
        deltas[1].wait()
        sums.wait()

    def pair(k, carry):
        a = 2 * k
        cols = jnp.concatenate([window(ext, r, a), window(ext, r, a + 1)], axis=1)
        rows = jnp.concatenate([shifted(d_ref[g, a]), shifted(d_ref[g, a + 1])], axis=1)
        acc[...] += lax.dot_general(rows, cols, (((1,), (1,)), ((), ())),
                                    preferred_element_type=f32)
        return carry

    lax.fori_loop(0, na // 2, pair, 0)

    def tiles(low, high):
        for s in range(4):
            first = 24 * ((place[2] + s) % 4)
            for b in range(3):
                rows = pl.ds(pl.multiple_of(first + 8 * b, 8), 8)
                for l in range(21):
                    n = b * 21 + l
                    (low if n < 32 else high)[s, n % 32] = (
                        flat[rows, 128 * l : 128 * l + 128] * inverse_scale
                    ).astype(bf16)
            high[s, 31] = jnp.zeros((8, 128), bf16)

    @pl.when(g == 1)
    def _():
        flat[:, 27 * c :] = jnp.zeros((c, flat.shape[1] - 27 * c), f32)
        for ij in range(9):
            for k in range(3):
                t = 3 * ij + k
                flat[:, t * c : (t + 1) * c] = acc[k * c : (k + 1) * c, ij * c : (ij + 1) * c]
        flat[:, 27 * c : 27 * c + 1] = jnp.sum(bsum_ref[...], axis=1, keepdims=True)
        pl.when(p == 0)(lambda: tiles(keep_ref, send_ref))
        pl.when(p == 1)(lambda: tiles(send_ref, keep_ref))


def weight_terms(x, sides, ends, d_out, bsum, acc):
    _, na, c, z = x.shape
    half = shape((4, 32, 8, 128))
    return call(
        weight_body, 2, [x, *sides, *ends, d_out, bsum, acc],
        [ANY] * 8,
        [half, half], [full(half), full(half)],
        ext_scratch(na, c, z)[:2] + [pltpu.VMEM((3 * c, K9), f32),
                                     pltpu.VMEM((c, 21 * 128), f32),
                                     pltpu.VMEM(d_out.shape, bf16),
                                     pltpu.VMEM(bsum.shape, f32)],
        2500000000)


def backward_body(place, d_in, d_out, *refs):
    sides, ends = refs[:2], refs[2:4]
    w_ref, out_ref, ext, sems, w_buf, res = refs[4:]
    r = pl.program_id(0)
    _, na, c, z = d_in.shape
    Loader(ext, sems, place, [d_in, d_out], sides, ends, w_ref, w_buf).each(r)

    def pair(k, carry):
        a = 2 * k
        cols = jnp.concatenate([window(ext, r, a), window(ext, r, a + 1)], axis=1)
        both = jnp.dot(w_buf[...], cols, preferred_element_type=f32)
        for s in range(2):
            put_column(res, a + s, na, taps_sum(both[:, s * z : (s + 1) * z]))
        return carry

    lax.fori_loop(0, na // 2, pair, 0)
    out_ref[0, :, 0] = get_rows(res, c, na).astype(bf16)


def backward(d_in, d_out, sides, ends, w):
    _, na, c, z = d_in.shape
    args = [d_in, d_out, *sides, *ends, w]
    return call(
        backward_body, 4, args, [ANY] * len(args), shape((1, c, 4, na, z)),
        pl.BlockSpec((1, c, 1, na, z), lambda r: (0, 0, r, 0, 0)),
        ext_scratch(na, c, z) + [pltpu.VMEM((z // 128, c * na, 128), f32)], 5000000000)


def near_pairs(axis):
    return [(i, i ^ 1) for i in range(lax.axis_size(axis))]


def far_pairs(axis):
    n = lax.axis_size(axis)
    pairs = [(i, i - 1 if i % 2 == 0 else i + 1) for i in range(n)]
    if axis == "azi":
        return [(i, j % n) for i, j in pairs]
    return [(i, j) for i, j in pairs if 0 <= j < n]


def swap(x, axis):
    near, far = x
    got_far = lax.ppermute(far, axis, far_pairs(axis))
    got_near = lax.ppermute(near, axis, near_pairs(axis))
    return got_near, got_far


def sum_over(x, axis, step):
    n = lax.axis_size(axis)
    parts = [x] + [
        lax.ppermute(x, axis, [(i, (i + step * s) % n) for i in range(n)]) for s in (1, 2, 3)
    ]
    a, b, c, d = (y.astype(f32) for y in parts)
    return (a + c) + (b + d)


def reduce_terms(keep, send):
    core = [(i, i ^ 1) for i in range(lax.axis_size("azi"))]
    got = lax.ppermute(send, "azi", core)
    mine = [keep[s].astype(f32) + got[s].astype(f32) for s in range(4)]
    total = mine[0]
    for s in (1, 2, 3):
        y = lax.ppermute(mine[s].astype(bf16), "dp", [(i, (i + s) % 4) for i in range(4)])
        total = total + y.astype(f32)
    n = lax.axis_size("rad")
    total = total.astype(bf16)
    y = lax.ppermute(total, "rad", [(i, i ^ 2) for i in range(n)])
    total = (total.astype(f32) + y.astype(f32)).astype(bf16)
    a, b, c = (
        lax.ppermute(total, "rad", [(i, i ^ step) for i in range(n)]) for step in (1, 4, 5)
    )
    a, b, c, d = (y.astype(f32) for y in (a, b, c, total))
    total = (d + a) + (b + c)
    total = sum_over(total.astype(bf16), "azi", 2)
    y = lax.ppermute(total, "azi", core)
    low = lax.axis_index("azi") % 2 == 0
    return jnp.concatenate([jnp.where(low, total, y), jnp.where(low, y, total)], axis=0)


def whole_weights(weight, bias):
    rows, width = weight.shape
    packed = jnp.concatenate([weight, jnp.broadcast_to(bias[:, None], (rows, 128))], axis=1)
    pieces = [packed] + [
        lax.ppermute(packed, "dp", [(i, (i + s) % 4) for i in range(4)]) for s in (1, 2, 3)
    ]
    order = (lax.axis_index("dp") - jnp.arange(4)) % 4
    whole = jnp.stack(pieces)[order].reshape(4 * rows, packed.shape[1])
    taps = whole[:, :width].reshape(4 * rows, 3, 3, 3, C)
    w_fwd = taps.transpose(3, 0, 1, 2, 4).reshape(3 * C, K9)
    w_back = taps[:, ::-1, ::-1, ::-1].transpose(3, 4, 1, 2, 0).reshape(3 * C, K9)
    return w_fwd, w_back, whole[:, width : width + 128]


def on_device(inputs, weight, bias, cotangent):
    x, near_face, far_face, near_row, far_row = to_columns(inputs)
    sides = swap((near_face, far_face), "azi")
    ends = swap(insert(0, (near_row, far_row), sides), "rad")
    w_fwd, w_back, b_col = whole_weights(weight, bias)
    out, d_in, near_in, far_in, bsum, acc = forward(
        x, sides, (), w_fwd, b_col, cotangent)
    output, d_out, near_face, far_face, bsum, d_near, d_far = forward(
        x, sides, ends, w_fwd, b_col, cotangent, [out, near_in, far_in, bsum])
    d_ends = swap((d_near, d_far), "rad")
    keep, send = weight_terms(x, sides, ends, d_out, bsum, acc)
    d_sides = swap(insert(1, (near_face, far_face), d_ends), "azi")
    tiles = reduce_terms(keep, send)
    input_grad = backward(d_in, d_out, d_sides, d_ends, w_back)
    summed = tiles[:63].reshape(3, 21, 8, 128).transpose(0, 2, 1, 3).reshape(24, 21 * 128)
    return output, input_grad, summed[:, : 27 * C], summed[:, 27 * C]


def solution(mesh):
    return jax.shard_map(
        on_device,
        mesh=mesh,
        in_specs=(
            P("dp", None, "rad", "azi", None),
            P("dp", None),
            P("dp"),
            P("dp", None, "rad", "azi", None),
        ),
        out_specs=(
            P("dp", None, "rad", "azi", None),
            P("dp", None, "rad", "azi", None),
            P("dp", None),
            P("dp"),
        ),
        check_vma=False,
    )
```
